128 devices in a mesh: site: 128 (over x, z, y, core).
Axes of the slice: x: 4, y: 4, z: 4, core: 2. Of those that a mesh axis runs over, the one named last changes fastest.
Arguments:
- site_tensors: bfloat16 [128, 256, 8, 256], P('site'), may hold values from -1.5 to 1.5
- first_gates: bfloat16 [128, 64, 64], P('site'), may hold values from -0.75 to 0.75
- second_gates: bfloat16 [128, 64, 64], P('site'), may hold values from -0.75 to 0.75
- first_sketch: int32 [128, 2048, 256], P('site'), may hold values from -1 to 1
- second_sketch: int32 [128, 2048, 256], P('site'), may hold values from -1 to 1
Outputs:
- evolved: bfloat16 [128, 256, 8, 256], P('site')
The draws below stay inside these ranges and needn't reach their ends.
All inputs are finite; a program needn't handle non-finite values.
Results may differ from the reference program's by a relative error of at most 0.018.
Values may be sent and summed in bfloat16 or wider, within the bound.
No kernel may reach another device: no remote copies, remote signals or barrier semaphores. Data moves between devices by JAX's collectives and lax.ppermute only.
A program may use at most 64 MiB of HBM per device.

```python
import jax
import jax.numpy as jnp
from jax import lax

CHI = 256
LEVELS = 8
SITES = 128


def place_ends(entries, key, low, largest):
    longest = entries.shape.index(max(entries.shape))
    spots = []
    for shift in (0, 1):
        where = [jax.random.randint(jax.random.fold_in(key, axis), (), 0, length) for axis, length in enumerate(entries.shape)]
        where[longest] = (where[longest] + shift) % entries.shape[longest]
        spots.append(tuple(where))
    return entries.at[spots[0]].set(low).at[spots[1]].set(largest)


def block_scale(own_key, extent, split, smallest, high):
    def one(dim, parts):
        steps = jax.random.uniform(jax.random.fold_in(jax.random.fold_in(own_key, 6), dim), (parts,), jnp.float32, smallest / len(split), high / len(split))
        return jnp.repeat(jnp.exp(steps), extent[dim] // parts).reshape((-1,) + (1,) * (len(extent) - dim - 1))

    gain = one(*split[0])
    for cut in split[1:]:
        gain = gain * one(*cut)
    return gain


def normal_values(key, dims, scale, most, shards=(), kind=jnp.bfloat16):
    loudness = block_scale(key, dims, shards, -0.22, 0.18) if shards else 1.0
    values = jax.random.normal(key, dims, jnp.float32) * scale * loudness
    return jnp.minimum(jnp.maximum(values, -most), most).astype(kind)


def setup_inputs(seed: int = 0) -> dict:
    seeds = jax.random.split(jax.random.key(seed), 6)
    site_tensors = normal_values(seeds[0], (SITES, CHI, LEVELS, CHI), (CHI ** 0.5) ** -0.5, 1.5, ((0, 128),))
    first_gates = normal_values(seeds[1], (SITES, LEVELS * LEVELS, LEVELS * LEVELS), (LEVELS * LEVELS) ** -0.5, 0.75, ((0, 128),))
    second_gates = normal_values(seeds[2], (SITES, LEVELS * LEVELS, LEVELS * LEVELS), (LEVELS * LEVELS) ** -0.5, 0.75, ((0, 128),))
    first_sketch = place_ends(jax.random.randint(seeds[3], (SITES, LEVELS * CHI, CHI), -1, 2), jax.random.fold_in(seeds[3], 1), -1, 1).astype(jnp.int32)
    second_sketch = place_ends(jax.random.randint(seeds[4], (SITES, LEVELS * CHI, CHI), -1, 2), jax.random.fold_in(seeds[4], 1), -1, 1).astype(jnp.int32)
    return {"site_tensors": site_tensors, "first_gates": first_gates, "second_gates": second_gates, "first_sketch": first_sketch, "second_sketch": second_sketch}


def update_pair(left_tensor, right_tensor, gate_matrix, sketch_matrix):
    two_site = jnp.dot(left_tensor.reshape(CHI * LEVELS, CHI).astype(jnp.float32), right_tensor.reshape(CHI, LEVELS * CHI).astype(jnp.float32), preferred_element_type=jnp.float32).astype(jnp.bfloat16)
    two_site = two_site.reshape(CHI, LEVELS * LEVELS, CHI)
    gated_pair = jnp.einsum('xy,ayc->axc', gate_matrix.astype(jnp.float32), two_site.astype(jnp.float32)).astype(jnp.bfloat16)
    matrix = gated_pair.reshape(CHI * LEVELS, LEVELS * CHI)
    sampled = jnp.dot(matrix.astype(jnp.float32), sketch_matrix.astype(jnp.bfloat16).astype(jnp.float32), preferred_element_type=jnp.float32)
    gram_matrix = jnp.dot(sampled.T, sampled, precision=lax.Precision.HIGHEST)
    factor_lower = jnp.linalg.cholesky(gram_matrix)
    basis_rows = jax.scipy.linalg.solve_triangular(factor_lower, sampled.T, lower=True)
    new_left = (basis_rows.T * (LEVELS ** 0.5 * CHI ** 0.25)).astype(jnp.bfloat16)
    product = lax.dot_general(new_left.astype(jnp.float32), matrix.astype(jnp.float32), (((0,), (0,)), ((), ())), preferred_element_type=jnp.float32)
    new_right = (product * (LEVELS * CHI) ** (-0.5)).astype(jnp.bfloat16)
    return (new_left.reshape(CHI, LEVELS, CHI), new_right.reshape(CHI, LEVELS, CHI))

def apply_layer(tensors, gates, sketches, parity):

    def advance(pair_index, current):
        left_index = (parity + 2 * pair_index).astype(jnp.int32)
        right_index = jnp.minimum(left_index + 1, SITES - 1).astype(jnp.int32)
        inside = left_index + 1 < SITES
        left_tensor = lax.dynamic_index_in_dim(current, left_index, 0, keepdims=False)
        right_tensor = lax.dynamic_index_in_dim(current, right_index, 0, keepdims=False)
        gate_matrix = lax.dynamic_index_in_dim(gates, left_index, 0, keepdims=False)
        sketch_matrix = lax.dynamic_index_in_dim(sketches, left_index, 0, keepdims=False)
        new_left, new_right = update_pair(left_tensor, right_tensor, gate_matrix, sketch_matrix)
        new_left = jnp.where(inside, new_left, left_tensor)
        new_right = jnp.where(inside, new_right, right_tensor)
        current = lax.dynamic_update_index_in_dim(current, new_right, right_index, 0)
        current = lax.dynamic_update_index_in_dim(current, new_left, left_index, 0)
        return current
    return lax.fori_loop(0, SITES // 2, advance, tensors)

def reference(site_tensors, first_gates, second_gates, first_sketch, second_sketch):
    tensors = apply_layer(site_tensors, first_gates, first_sketch, 0)
    tensors = apply_layer(tensors, second_gates, second_sketch, 1)
    return tensors
```

```python
import functools

import jax
import jax.numpy as jnp
from jax import lax
from jax.experimental import pallas as pl
from jax.experimental.pallas import tpu as pltpu
from jax.sharding import PartitionSpec as P

F32 = jnp.float32
BF16 = jnp.bfloat16
ANY = pl.BlockSpec(memory_space=pl.ANY)
VMEM = pl.BlockSpec(memory_space=pltpu.VMEM)
CHI = 256
LEVELS = 8
ROWS = CHI * LEVELS
GATE = LEVELS * LEVELS
BLOCK = 64


def lanes_of(v, k):
    return jnp.broadcast_to(v[:, k : k + 1], (8, 128))


def row_of(v, r):
    return jnp.broadcast_to(v[r : r + 1, :], (8, 128))


def inverse_factor(diag_block):
    nb = BLOCK
    nv = nb // 8
    rows = lax.broadcasted_iota(jnp.int32, (nb, nb), 0)
    cols = lax.broadcasted_iota(jnp.int32, (nb, nb), 1)
    beside = jnp.concatenate([diag_block, jnp.where(rows == cols, 1.0, 0.0).astype(F32)], axis=1)
    v = [beside[8 * q : 8 * q + 8, :] for q in range(nv)]
    sub = lax.broadcasted_iota(jnp.int32, (8, 128), 0)
    scale = [jnp.ones((8, 128), F32)] * nv
    c = [[lanes_of(v[q], i) for q in range(nv)] for i in range(4)]
    for k in range(0, nb, 4):
        p, r = divmod(k, 8)
        last = k + 4 >= nb
        if not last:
            p2, r2 = divmod(k + 4, 8)
            ahead = [[lanes_of(v[q], k + 4 + i) for q in range(p2, nv)] for i in range(4)]
        row = [row_of(v[p], r + i) for i in range(4)]
        g = [[row_of(c[j][0], r + i) if i >= j else None for j in range(4)] for i in range(4)]
        a, b, d = g[0][0], g[1][0], g[1][1]
        det = a * d - b * b
        idet = 1.0 / det
        ia = 1.0 / a
        ad, bd, dd = a * idet, b * idet, d * idet

        def first_pair(x, y):
            return x * dd - y * bd, y * ad - x * bd

        m20, m21 = first_pair(g[2][0], g[2][1])
        m30, m31 = first_pair(g[3][0], g[3][1])
        a2 = g[2][2] - (m20 * g[2][0] + m21 * g[2][1])
        b2 = g[3][2] - (m30 * g[2][0] + m31 * g[2][1])
        d2 = g[3][3] - (m30 * g[3][0] + m31 * g[3][1])
        det2 = a2 * d2 - b2 * b2
        idet2 = 1.0 / det2
        ia2 = 1.0 / a2
        ad2, bd2, dd2 = a2 * idet2, b2 * idet2, d2 * idet2

        def panel_solve(x0, x1, x2, x3):
            y2 = x2 - (m20 * x0 + m21 * x1)
            y3 = x3 - (m30 * x0 + m31 * x1)
            h2 = y2 * dd2 - y3 * bd2
            h3 = y3 * ad2 - y2 * bd2
            u0, u1 = first_pair(x0, x1)
            return (u0 - (m20 * h2 + m30 * h3), u1 - (m21 * h2 + m31 * h3), h2, h3), y2, y3

        if not last:
            c_next = []
            for i in range(4):
                hs, _, _ = panel_solve(*[row_of(c[j][p2 - p], r2 + i) for j in range(4)])
                c_next.append(
                    [
                        ahead[i][q - p2]
                        - (
                            (c[0][q - p] * hs[0] + c[1][q - p] * hs[1])
                            + (c[2][q - p] * hs[2] + c[3][q - p] * hs[3])
                        )
                        for q in range(p2, nv)
                    ]
                )
        h, row2, row3 = panel_solve(*row)
        below = sub > r + 3
        for q in range(p, nv):
            cq = [c[j][q - p] for j in range(4)]
            if q == p:
                cq = [jnp.where(below, x, 0.0) for x in cq]
            v[q] = v[q] - ((cq[0] * h[0] + cq[1] * h[1]) + (cq[2] * h[2] + cq[3] * h[3]))
        row1 = row[1] - (b * ia) * row[0]
        row3 = row3 - (b2 * ia2) * row2
        v[p] = jnp.where(
            sub == r + 1, row1, jnp.where(sub == r + 2, row2, jnp.where(sub == r + 3, row3, v[p]))
        )
        scale[p] = jnp.where(
            sub == r,
            lax.rsqrt(a),
            jnp.where(
                sub == r + 1,
                lax.rsqrt(det * ia),
                jnp.where(sub == r + 2, lax.rsqrt(a2), jnp.where(sub == r + 3, lax.rsqrt(det2 * ia2), scale[p])),
            ),
        )
        if not last:
            c = c_next
    return jnp.concatenate([v[q] * scale[q] for q in range(nv)], axis=0)[:, nb:]


def dot(x, y, dims=((1,), (0,))):
    return lax.dot_general(x, y, (dims, ((), ())), preferred_element_type=F32)


def dot_split(x, y, dims=((1,), (0,))):
    xh = x.astype(BF16)
    xl = (x - xh.astype(F32)).astype(BF16)
    yh = y.astype(BF16)
    yl = (y - yh.astype(F32)).astype(BF16)
    return dot(xh, yh, dims) + (dot(xh, yl, dims) + dot(xl, yh, dims))


def gate_matrix(packed):
    i = lax.broadcasted_iota(jnp.int32, (GATE, GATE), 0)
    j = lax.broadcasted_iota(jnp.int32, (GATE, GATE), 1)
    swap = jnp.where(j == (i & 7) * 8 + (i >> 3), 1.0, 0.0).astype(BF16)
    g = dot(dot(swap, packed[:, :GATE]).astype(BF16), swap, ((1,), (1,))).astype(BF16)
    wide = jnp.concatenate([jnp.concatenate([g] * 4, axis=1)] * 4, axis=0)
    big_i = lax.broadcasted_iota(jnp.int32, (4 * GATE, 4 * GATE), 0)
    big_j = lax.broadcasted_iota(jnp.int32, (4 * GATE, 4 * GATE), 1)
    return jnp.where((big_i >> 6) == (big_j >> 6), wide, jnp.zeros_like(wide))


def every_level(wide, t):
    return jnp.concatenate([wide[h, pl.ds(t, CHI, stride=LEVELS), :] for h in range(2)], axis=1)


def put_level(wide, t, value):
    for h in range(2):
        wide[h, pl.ds(t, CHI, stride=LEVELS), :] = value[:, h * 128 : (h + 1) * 128]


def pair_kernel(own, recv, sk_own, sk_recv, out, left, right, raw, sk, gate, y, m, s, wide, q, ab, sems, *, layer):
    me = lax.axis_index("site")
    devices = lax.axis_size("site")
    is_left = lax.rem(me, 2) == layer
    idle = (layer == 1) & ((me == 0) | (me == devices - 1))
    right_in = raw if layer == 0 else right

    @pl.when(is_left)
    def _():
        pltpu.make_async_copy(recv, right_in, sems.at[1]).start()
        pltpu.make_async_copy(own, left, sems.at[0]).start()
        pltpu.make_async_copy(sk_own, sk, sems.at[2]).start()

    @pl.when(jnp.logical_not(is_left))
    def _():
        pltpu.make_async_copy(own, right_in, sems.at[1]).start()
        pltpu.make_async_copy(recv, left, sems.at[0]).start()
        pltpu.make_async_copy(sk_recv, sk, sems.at[2]).start()

    pltpu.make_async_copy(own, right_in, sems.at[1]).wait()
    if layer == 0:
        for h in range(2):
            wide[h] = raw[:, h * 128 : (h + 1) * 128].astype(F32)
        for t in range(LEVELS):
            right[t * CHI : (t + 1) * CHI, :] = every_level(wide, t).astype(BF16)
    pltpu.make_async_copy(own, left, sems.at[0]).wait()

    step = 1024
    bonds = step // LEVELS

    def two_site(i, _):
        r0 = pl.multiple_of(i * step, step)
        a0 = pl.multiple_of(i * bonds, bonds)
        block = left[pl.ds(r0, step), :]
        for t in range(0, LEVELS, 2):
            parts = [
                dot(block, right[u * CHI : (u + 1) * CHI, :]).reshape(bonds, LEVELS, CHI) for u in (t, t + 1)
            ]
            y[pl.ds(a0, bonds), t * LEVELS : (t + 2) * LEVELS, :] = jnp.concatenate(parts, axis=1).astype(BF16)
        return 0

    lax.fori_loop(0, ROWS // step, two_site, 0)

    pltpu.make_async_copy(sk_own, sk, sems.at[2]).wait()
    gate[...] = gate_matrix(sk[ROWS:, :])

    step_g = 512
    bonds_g = step_g // LEVELS

    def gated(i, _):
        r0 = pl.multiple_of(i * step_g, step_g)
        a0 = pl.multiple_of(i * bonds_g, bonds_g)
        for j in range(bonds_g // 4):
            four = y[pl.ds(a0 + 4 * j, 4)].reshape(4 * GATE, CHI)
            o = dot(gate[...], four).reshape(4, LEVELS, LEVELS, CHI)
            for h in range(2):
                at = pl.multiple_of(r0 + j * 32 + h * 16, 16)
                for t in range(LEVELS):
                    m[pl.ds(at, 16), t * CHI : (t + 1) * CHI] = jnp.concatenate(
                        [o[2 * h, t], o[2 * h + 1, t]], axis=0
                    ).astype(BF16)
        return 0

    lax.fori_loop(0, ROWS // step_g, gated, 0)

    def sample(i, _):
        r0 = pl.multiple_of(i * step, step)
        s[pl.ds(r0, step), :] = dot(m[pl.ds(r0, step), :], sk[:ROWS, :]).astype(BF16)
        return 0

    lax.fori_loop(0, ROWS // step, sample, 0)

    ab[:, :CHI] = dot(s[...], s[...], ((0,), (0,)))
    diag_i = lax.broadcasted_iota(jnp.int32, (CHI, CHI), 0)
    diag_j = lax.broadcasted_iota(jnp.int32, (CHI, CHI), 1)
    ab[:, CHI:] = jnp.where(diag_i == diag_j, 1.0, 0.0).astype(F32)
    for o in range(0, CHI, BLOCK):
        e = o + BLOCK
        w = inverse_factor(ab[o:e, o:e])
        panel = dot_split(w, ab[o:e, :])
        ab[o:e, CHI:] = panel[:, CHI:]
        if e < CHI:
            ab[e:, :] = ab[e:, :] - dot_split(panel[:, e:CHI], panel, ((0,), (0,)))

    left_scale = LEVELS**0.5 * CHI**0.25

    @pl.when(is_left)
    def _():
        inv = (ab[:, CHI:] * left_scale).astype(BF16)
        if layer == 0:
            made = dot(s[...], inv, ((1,), (1,)))
            for h in range(2):
                wide[h] = made[:, h * 128 : (h + 1) * 128]
            for t in range(LEVELS):
                out[t * CHI : (t + 1) * CHI, :] = every_level(wide, t).astype(BF16)
        else:
            out[...] = dot(s[...], inv, ((1,), (1,))).astype(BF16)

            @pl.when(idle)
            def _():
                out[...] = left[...]

    @pl.when(jnp.logical_not(is_left))
    def _():
        inv = (ab[:, CHI:] * (left_scale * ROWS**-0.5)).astype(BF16)
        for t in range(LEVELS):
            q[...] = dot(s[...], m[:, t * CHI : (t + 1) * CHI], ((0,), (0,)))
            put_level(wide, t, dot(inv, q[...].astype(BF16)))
        if layer == 1:

            @pl.when(idle)
            def _():
                for t in range(LEVELS):
                    put_level(wide, t, right[t * CHI : (t + 1) * CHI, :].astype(F32))

        for h in range(2):
            out[:, h * 128 : (h + 1) * 128] = wide[h].astype(BF16)


def pair_step(own, recv, sk_own, sk_recv, layer):
    return pl.pallas_call(
        functools.partial(pair_kernel, layer=layer),
        out_shape=jax.ShapeDtypeStruct((ROWS, CHI), BF16),
        in_specs=[ANY] * 4,
        out_specs=VMEM,
        scratch_shapes=[
            pltpu.VMEM((ROWS, CHI), BF16),
            pltpu.VMEM((ROWS, CHI), BF16),
            pltpu.VMEM((ROWS, CHI), BF16),
            pltpu.VMEM((ROWS + GATE, CHI), BF16),
            pltpu.VMEM((4 * GATE, 4 * GATE), BF16),
            pltpu.VMEM((CHI, GATE, CHI), BF16),
            pltpu.VMEM((ROWS, ROWS), BF16),
            pltpu.VMEM((ROWS, CHI), BF16),
            pltpu.VMEM((2, ROWS, 128), F32),
            pltpu.VMEM((CHI, CHI), F32),
            pltpu.VMEM((CHI, 2 * CHI), F32),
            pltpu.SemaphoreType.DMA((3,)),
        ],
        compiler_params=pltpu.CompilerParams(vmem_limit_bytes=56 << 20),
        name=f"pair{layer}",
    )(own, recv, sk_own, sk_recv)


def pack_kernel(sketch, gate, out):
    out[:ROWS, :] = sketch[...].astype(BF16)
    out[ROWS:, :] = jnp.concatenate([gate[...]] * 4, axis=1)


def pack(sketch, gate, layer):
    return pl.pallas_call(
        pack_kernel,
        out_shape=jax.ShapeDtypeStruct((ROWS + GATE, CHI), BF16),
        in_specs=[VMEM, VMEM],
        out_specs=VMEM,
        name=f"pack{layer}",
    )(sketch, gate)


def per_device(site_tensors, first_gates, second_gates, first_sketch, second_sketch):
    devices = lax.axis_size("site")
    inside = [(i, i ^ 1) for i in range(devices)]
    across = [(i, (i + 1) % devices if i % 2 else (i - 1) % devices) for i in range(devices)]
    own = site_tensors[0].reshape(ROWS, CHI)
    recv = lax.ppermute(own, "site", inside)
    sk0 = pack(first_sketch[0], first_gates[0], 0)
    sk0_recv = lax.ppermute(sk0, "site", inside)
    sk1 = pack(second_sketch[0], second_gates[0], 1)
    sk1_recv = lax.ppermute(sk1, "site", across)
    own = pair_step(own, recv, sk0, sk0_recv, 0)
    recv = lax.ppermute(own, "site", across)
    own = pair_step(own, recv, sk1, sk1_recv, 1)
    return own.reshape(1, CHI, LEVELS, CHI)


def solution(mesh):
    in_specs = (
        P("site", None, None, None),
        P("site", None, None),
        P("site", None, None),
        P("site", None, None),
        P("site", None, None),
    )
    out_specs = P("site", None, None, None)
    return jax.shard_map(
        per_device, mesh=mesh, in_specs=in_specs, out_specs=out_specs, check_vma=False
    )
```

```python
import functools

import jax
import jax.numpy as jnp
from jax import lax
from jax.experimental import pallas as pl
from jax.experimental.pallas import tpu as pltpu
from jax.sharding import PartitionSpec as P

F32 = jnp.float32
BF16 = jnp.bfloat16
ANY = pl.BlockSpec(memory_space=pl.ANY)
VMEM = pl.BlockSpec(memory_space=pltpu.VMEM)
CHI = 256
LEVELS = 8
ROWS = CHI * LEVELS
GATE = LEVELS * LEVELS
BLOCK = 64


def lanes_of(v, k):
    return jnp.broadcast_to(v[:, k : k + 1], (8, 128))


def row_of(v, r):
    return jnp.broadcast_to(v[r : r + 1, :], (8, 128))


def inverse_factor(diag_block):
    nb = BLOCK
    nv = nb // 8
    rows = lax.broadcasted_iota(jnp.int32, (nb, nb), 0)
    cols = lax.broadcasted_iota(jnp.int32, (nb, nb), 1)
    beside = jnp.concatenate([diag_block, jnp.where(rows == cols, 1.0, 0.0).astype(F32)], axis=1)
    v = [beside[8 * q : 8 * q + 8, :] for q in range(nv)]
    sub = lax.broadcasted_iota(jnp.int32, (8, 128), 0)
    scale = [jnp.ones((8, 128), F32)] * nv
    c = [[lanes_of(v[q], i) for q in range(nv)] for i in range(4)]
    for k in range(0, nb, 4):
        p, r = divmod(k, 8)
        last = k + 4 >= nb
        if not last:
            p2, r2 = divmod(k + 4, 8)
            ahead = [[lanes_of(v[q], k + 4 + i) for q in range(p2, nv)] for i in range(4)]
        row = [row_of(v[p], r + i) for i in range(4)]
        g = [[row_of(c[j][0], r + i) if i >= j else None for j in range(4)] for i in range(4)]
        a, b, d = g[0][0], g[1][0], g[1][1]
        det = a * d - b * b
        idet = 1.0 / det
        ia = 1.0 / a
        ad, bd, dd = a * idet, b * idet, d * idet

        def first_pair(x, y):
            return x * dd - y * bd, y * ad - x * bd

        m20, m21 = first_pair(g[2][0], g[2][1])
        m30, m31 = first_pair(g[3][0], g[3][1])
        a2 = g[2][2] - (m20 * g[2][0] + m21 * g[2][1])
        b2 = g[3][2] - (m30 * g[2][0] + m31 * g[2][1])
        d2 = g[3][3] - (m30 * g[3][0] + m31 * g[3][1])
        det2 = a2 * d2 - b2 * b2
        idet2 = 1.0 / det2
        ia2 = 1.0 / a2
        ad2, bd2, dd2 = a2 * idet2, b2 * idet2, d2 * idet2

        def panel_solve(x0, x1, x2, x3):
            y2 = x2 - (m20 * x0 + m21 * x1)
            y3 = x3 - (m30 * x0 + m31 * x1)
            h2 = y2 * dd2 - y3 * bd2
            h3 = y3 * ad2 - y2 * bd2
            u0, u1 = first_pair(x0, x1)
            return (u0 - (m20 * h2 + m30 * h3), u1 - (m21 * h2 + m31 * h3), h2, h3), y2, y3

        if not last:
            c_next = []
            for i in range(4):
                hs, _, _ = panel_solve(*[row_of(c[j][p2 - p], r2 + i) for j in range(4)])
                c_next.append(
                    [
                        ahead[i][q - p2]
                        - (
                            (c[0][q - p] * hs[0] + c[1][q - p] * hs[1])
                            + (c[2][q - p] * hs[2] + c[3][q - p] * hs[3])
                        )
                        for q in range(p2, nv)
                    ]
                )
        h, row2, row3 = panel_solve(*row)
        below = sub > r + 3
        for q in range(p, nv):
            cq = [c[j][q - p] for j in range(4)]
            if q == p:
                cq = [jnp.where(below, x, 0.0) for x in cq]
            v[q] = v[q] - ((cq[0] * h[0] + cq[1] * h[1]) + (cq[2] * h[2] + cq[3] * h[3]))
        row1 = row[1] - (b * ia) * row[0]
        row3 = row3 - (b2 * ia2) * row2
        v[p] = jnp.where(
            sub == r + 1, row1, jnp.where(sub == r + 2, row2, jnp.where(sub == r + 3, row3, v[p]))
        )
        scale[p] = jnp.where(
            sub == r,
            lax.rsqrt(a),
            jnp.where(
                sub == r + 1,
                lax.rsqrt(det * ia),
                jnp.where(sub == r + 2, lax.rsqrt(a2), jnp.where(sub == r + 3, lax.rsqrt(det2 * ia2), scale[p])),
            ),
        )
        if not last:
            c = c_next
    return jnp.concatenate([v[q] * scale[q] for q in range(nv)], axis=0)[:, nb:]


def dot(x, y, dims=((1,), (0,))):
    return lax.dot_general(x, y, (dims, ((), ())), preferred_element_type=F32)


def dot_split(x, y, dims=((1,), (0,))):
    xh = x.astype(BF16)
    xl = (x - xh.astype(F32)).astype(BF16)
    yh = y.astype(BF16)
    yl = (y - yh.astype(F32)).astype(BF16)
    return dot(xh, yh, dims) + (dot(xh, yl, dims) + dot(xl, yh, dims))


def gate_matrix(packed):
    i = lax.broadcasted_iota(jnp.int32, (GATE, GATE), 0)
    j = lax.broadcasted_iota(jnp.int32, (GATE, GATE), 1)
    swap = jnp.where(j == (i & 7) * 8 + (i >> 3), 1.0, 0.0).astype(BF16)
    g = dot(dot(swap, packed[:, :GATE]).astype(BF16), swap, ((1,), (1,))).astype(BF16)
    wide = jnp.concatenate([jnp.concatenate([g] * 4, axis=1)] * 4, axis=0)
    big_i = lax.broadcasted_iota(jnp.int32, (4 * GATE, 4 * GATE), 0)
    big_j = lax.broadcasted_iota(jnp.int32, (4 * GATE, 4 * GATE), 1)
    return jnp.where((big_i >> 6) == (big_j >> 6), wide, jnp.zeros_like(wide))


def every_level(wide, t):
    return jnp.concatenate([wide[h, pl.ds(t, CHI, stride=LEVELS), :] for h in range(2)], axis=1)


def put_level(wide, t, value):
    for h in range(2):
        wide[h, pl.ds(t, CHI, stride=LEVELS), :] = value[:, h * 128 : (h + 1) * 128]


def pair_kernel(own, recv, sk_own, sk_recv, out, left, right, raw, sk, gate, y, m, s, st, wide, q, ab, sems, *, layer):
    me = lax.axis_index("site")
    devices = lax.axis_size("site")
    is_left = lax.rem(me, 2) == layer
    idle = (layer == 1) & ((me == 0) | (me == devices - 1))
    right_in = raw if layer == 0 else right

    @pl.when(is_left)
    def _():
        pltpu.make_async_copy(recv, right_in, sems.at[1]).start()
        pltpu.make_async_copy(own, left, sems.at[0]).start()
        pltpu.make_async_copy(sk_own, sk, sems.at[2]).start()

    @pl.when(jnp.logical_not(is_left))
    def _():
        pltpu.make_async_copy(own, right_in, sems.at[1]).start()
        pltpu.make_async_copy(recv, left, sems.at[0]).start()
        pltpu.make_async_copy(sk_recv, sk, sems.at[2]).start()

    pltpu.make_async_copy(own, right_in, sems.at[1]).wait()
    if layer == 0:
        for h in range(2):
            wide[h] = raw[:, h * 128 : (h + 1) * 128].astype(F32)
        for t in range(LEVELS):
            right[t * CHI : (t + 1) * CHI, :] = every_level(wide, t).astype(BF16)
    pltpu.make_async_copy(own, left, sems.at[0]).wait()

    step = 1024
    bonds = step // LEVELS

    def two_site(i, _):
        r0 = pl.multiple_of(i * step, step)
        a0 = pl.multiple_of(i * bonds, bonds)
        block = left[pl.ds(r0, step), :]
        for t in range(0, LEVELS, 2):
            parts = [
                dot(block, right[u * CHI : (u + 1) * CHI, :]).reshape(bonds, LEVELS, CHI) for u in (t, t + 1)
            ]
            y[pl.ds(a0, bonds), t * LEVELS : (t + 2) * LEVELS, :] = jnp.concatenate(parts, axis=1).astype(BF16)
        return 0

    lax.fori_loop(0, ROWS // step, two_site, 0)

    pltpu.make_async_copy(sk_own, sk, sems.at[2]).wait()
    gate[...] = gate_matrix(sk[ROWS:, :])

    step_g = 512
    bonds_g = step_g // LEVELS

    def gated(i, _):
        r0 = pl.multiple_of(i * step_g, step_g)
        a0 = pl.multiple_of(i * bonds_g, bonds_g)
        for j in range(bonds_g // 4):
            four = y[pl.ds(a0 + 4 * j, 4)].reshape(4 * GATE, CHI)
            o = dot(gate[...], four).reshape(4, LEVELS, LEVELS, CHI)
            for h in range(2):
                at = pl.multiple_of(r0 + j * 32 + h * 16, 16)
                for t in range(LEVELS):
                    m[pl.ds(at, 16), t * CHI : (t + 1) * CHI] = jnp.concatenate(
                        [o[2 * h, t], o[2 * h + 1, t]], axis=0
                    ).astype(BF16)
        return 0

    lax.fori_loop(0, ROWS // step_g, gated, 0)

    def sample(i, _):
        r0 = pl.multiple_of(i * step, step)
        s[pl.ds(r0, step), :] = dot(m[pl.ds(r0, step), :], sk[:ROWS, :]).astype(BF16)
        return 0

    lax.fori_loop(0, ROWS // step, sample, 0)

    unit = jnp.where(
        lax.broadcasted_iota(jnp.int32, (CHI, CHI), 0) == lax.broadcasted_iota(jnp.int32, (CHI, CHI), 1), 1.0, 0.0
    ).astype(BF16)
    st[...] = dot(unit, s[...], ((1,), (1,))).astype(BF16)
    ab[:, :CHI] = dot(st[...], s[...])
    diag_i = lax.broadcasted_iota(jnp.int32, (CHI, CHI), 0)
    diag_j = lax.broadcasted_iota(jnp.int32, (CHI, CHI), 1)
    ab[:, CHI:] = jnp.where(diag_i == diag_j, 1.0, 0.0).astype(F32)
    for o in range(0, CHI, BLOCK):
        e = o + BLOCK
        w = inverse_factor(ab[o:e, o:e])
        for t in range(o // BLOCK * 2, o // BLOCK * 2 + 2):
            q[:, t * CHI : (t + 1) * CHI] = dot(st[...], m[:, t * CHI : (t + 1) * CHI]).astype(BF16)
        panel = dot_split(w, ab[o:e, :])
        ab[o:e, CHI:] = panel[:, CHI:]
        if e < CHI:
            ab[e:, :] = ab[e:, :] - dot_split(panel[:, e:CHI], panel, ((0,), (0,)))

    left_scale = LEVELS**0.5 * CHI**0.25

    @pl.when(is_left)
    def _():
        inv = (ab[:, CHI:] * left_scale).astype(BF16)
        if layer == 0:
            made = dot(s[...], inv, ((1,), (1,)))
            for h in range(2):
                wide[h] = made[:, h * 128 : (h + 1) * 128]
            for t in range(LEVELS):
                out[t * CHI : (t + 1) * CHI, :] = every_level(wide, t).astype(BF16)
        else:
            out[...] = dot(s[...], inv, ((1,), (1,))).astype(BF16)

            @pl.when(idle)
            def _():
                out[...] = left[...]

    @pl.when(jnp.logical_not(is_left))
    def _():
        inv = (ab[:, CHI:] * (left_scale * ROWS**-0.5)).astype(BF16)
        for t in range(LEVELS):
            put_level(wide, t, dot(inv, q[:, t * CHI : (t + 1) * CHI]))
        if layer == 1:

            @pl.when(idle)
            def _():
                for t in range(LEVELS):
                    put_level(wide, t, right[t * CHI : (t + 1) * CHI, :].astype(F32))

        for h in range(2):
            out[:, h * 128 : (h + 1) * 128] = wide[h].astype(BF16)


def pair_step(own, recv, sk_own, sk_recv, layer):
    return pl.pallas_call(
        functools.partial(pair_kernel, layer=layer),
        out_shape=jax.ShapeDtypeStruct((ROWS, CHI), BF16),
        in_specs=[ANY] * 4,
        out_specs=VMEM,
        scratch_shapes=[
            pltpu.VMEM((ROWS, CHI), BF16),
            pltpu.VMEM((ROWS, CHI), BF16),
            pltpu.VMEM((ROWS, CHI), BF16),
            pltpu.VMEM((ROWS + GATE, CHI), BF16),
            pltpu.VMEM((4 * GATE, 4 * GATE), BF16),
            pltpu.VMEM((CHI, GATE, CHI), BF16),
            pltpu.VMEM((ROWS, ROWS), BF16),
            pltpu.VMEM((ROWS, CHI), BF16),
            pltpu.VMEM((CHI, ROWS), BF16),
            pltpu.VMEM((2, ROWS, 128), F32),
            pltpu.VMEM((CHI, ROWS), BF16),
            pltpu.VMEM((CHI, 2 * CHI), F32),
            pltpu.SemaphoreType.DMA((3,)),
        ],
        compiler_params=pltpu.CompilerParams(vmem_limit_bytes=32 << 20),
        name=f"pair{layer}",
    )(own, recv, sk_own, sk_recv)


def pack(sketch, gate, layer):
    return jnp.concatenate([sketch.astype(BF16), jnp.concatenate([gate] * 4, axis=1)], axis=0)


def per_device(site_tensors, first_gates, second_gates, first_sketch, second_sketch):
    devices = lax.axis_size("site")
    inside = [(i, i ^ 1) for i in range(devices)]
    across = [(i, (i + 1) % devices if i % 2 else (i - 1) % devices) for i in range(devices)]
    own = site_tensors[0].reshape(ROWS, CHI)
    recv = lax.ppermute(own, "site", inside)
    sk0 = pack(first_sketch[0], first_gates[0], 0)
    sk0_recv = lax.ppermute(sk0, "site", inside)
    sk1 = pack(second_sketch[0], second_gates[0], 1)
    sk1_recv = lax.ppermute(sk1, "site", across)
    own = pair_step(own, recv, sk0, sk0_recv, 0)
    recv = lax.ppermute(own, "site", across)
    own = pair_step(own, recv, sk1, sk1_recv, 1)
    return own.reshape(1, CHI, LEVELS, CHI)


def solution(mesh):
    in_specs = (
        P("site", None, None, None),
        P("site", None, None),
        P("site", None, None),
        P("site", None, None),
        P("site", None, None),
    )
    out_specs = P("site", None, None, None)
    return jax.shard_map(
        per_device, mesh=mesh, in_specs=in_specs, out_specs=out_specs, check_vma=False
    )
```

```python
import jax
import jax.numpy as jnp
from jax import lax
from jax.experimental import pallas as pl
from jax.experimental.pallas import tpu as pltpu
from jax.sharding import PartitionSpec as P

F32 = jnp.float32
BF16 = jnp.bfloat16
ANY = pl.BlockSpec(memory_space=pl.ANY)
VMEM = pl.BlockSpec(memory_space=pltpu.VMEM)
CHI = 256
LEVELS = 8
ROWS = CHI * LEVELS
GATE = LEVELS * LEVELS
BLOCK = 64


def lanes_of(v, k):
    return jnp.broadcast_to(v[:, k : k + 1], (8, 128))


def row_of(v, r):
    return jnp.broadcast_to(v[r : r + 1, :], (8, 128))


def inverse_factor(diag_block):
    nb = BLOCK
    nv = nb // 8
    rows = lax.broadcasted_iota(jnp.int32, (nb, nb), 0)
    cols = lax.broadcasted_iota(jnp.int32, (nb, nb), 1)
    beside = jnp.concatenate([diag_block, jnp.where(rows == cols, 1.0, 0.0).astype(F32)], axis=1)
    v = [beside[8 * q : 8 * q + 8, :] for q in range(nv)]
    sub = lax.broadcasted_iota(jnp.int32, (8, 128), 0)
    scale = [jnp.ones((8, 128), F32)] * nv
    c = [[lanes_of(v[q], i) for q in range(nv)] for i in range(4)]
    for k in range(0, nb, 4):
        p, r = divmod(k, 8)
        last = k + 4 >= nb
        if not last:
            p2, r2 = divmod(k + 4, 8)
            ahead = [[lanes_of(v[q], k + 4 + i) for q in range(p2, nv)] for i in range(4)]
        row = [row_of(v[p], r + i) for i in range(4)]
        g = [[row_of(c[j][0], r + i) if i >= j else None for j in range(4)] for i in range(4)]
        a, b, d = g[0][0], g[1][0], g[1][1]
        det = a * d - b * b
        idet = 1.0 / det
        ia = 1.0 / a
        ad, bd, dd = a * idet, b * idet, d * idet

        def first_pair(x, y):
            return x * dd - y * bd, y * ad - x * bd

        m20, m21 = first_pair(g[2][0], g[2][1])
        m30, m31 = first_pair(g[3][0], g[3][1])
        a2 = g[2][2] - (m20 * g[2][0] + m21 * g[2][1])
        b2 = g[3][2] - (m30 * g[2][0] + m31 * g[2][1])
        d2 = g[3][3] - (m30 * g[3][0] + m31 * g[3][1])
        det2 = a2 * d2 - b2 * b2
        idet2 = 1.0 / det2
        ia2 = 1.0 / a2
        ad2, bd2, dd2 = a2 * idet2, b2 * idet2, d2 * idet2

        def panel_solve(x0, x1, x2, x3):
            y2 = x2 - (m20 * x0 + m21 * x1)
            y3 = x3 - (m30 * x0 + m31 * x1)
            h2 = y2 * dd2 - y3 * bd2
            h3 = y3 * ad2 - y2 * bd2
            u0, u1 = first_pair(x0, x1)
            return (u0 - (m20 * h2 + m30 * h3), u1 - (m21 * h2 + m31 * h3), h2, h3), y2, y3

        if not last:
            c_next = []
            for i in range(4):
                hs, _, _ = panel_solve(*[row_of(c[j][p2 - p], r2 + i) for j in range(4)])
                c_next.append(
                    [
                        ahead[i][q - p2]
                        - (
                            (c[0][q - p] * hs[0] + c[1][q - p] * hs[1])
                            + (c[2][q - p] * hs[2] + c[3][q - p] * hs[3])
                        )
                        for q in range(p2, nv)
                    ]
                )
        h, row2, row3 = panel_solve(*row)
        below = sub > r + 3
        for q in range(p, nv):
            cq = [c[j][q - p] for j in range(4)]
            if q == p:
                cq = [jnp.where(below, x, 0.0) for x in cq]
            v[q] = v[q] - ((cq[0] * h[0] + cq[1] * h[1]) + (cq[2] * h[2] + cq[3] * h[3]))
        row1 = row[1] - (b * ia) * row[0]
        row3 = row3 - (b2 * ia2) * row2
        v[p] = jnp.where(
            sub == r + 1, row1, jnp.where(sub == r + 2, row2, jnp.where(sub == r + 3, row3, v[p]))
        )
        scale[p] = jnp.where(
            sub == r,
            lax.rsqrt(a),
            jnp.where(
                sub == r + 1,
                lax.rsqrt(det * ia),
                jnp.where(sub == r + 2, lax.rsqrt(a2), jnp.where(sub == r + 3, lax.rsqrt(det2 * ia2), scale[p])),
            ),
        )
        if not last:
            c = c_next
    return jnp.concatenate([v[q] * scale[q] for q in range(nv)], axis=0)[:, nb:]


def dot(x, y, dims=((1,), (0,))):
    return lax.dot_general(x, y, (dims, ((), ())), preferred_element_type=F32)


def dot_split(x, y, dims=((1,), (0,))):
    xh = x.astype(BF16)
    xl = (x - xh.astype(F32)).astype(BF16)
    yh = y.astype(BF16)
    yl = (y - yh.astype(F32)).astype(BF16)
    return dot(xh, yh, dims) + (dot(xh, yl, dims) + dot(xl, yh, dims))


def gate_matrix(packed):
    i = lax.broadcasted_iota(jnp.int32, (GATE, GATE), 0)
    j = lax.broadcasted_iota(jnp.int32, (GATE, GATE), 1)
    swap = jnp.where(j == (i & 7) * 8 + (i >> 3), 1.0, 0.0).astype(BF16)
    g = dot(dot(swap, packed[:, :GATE]).astype(BF16), swap, ((1,), (1,))).astype(BF16)
    wide = jnp.concatenate([jnp.concatenate([g] * 4, axis=1)] * 4, axis=0)
    big_i = lax.broadcasted_iota(jnp.int32, (4 * GATE, 4 * GATE), 0)
    big_j = lax.broadcasted_iota(jnp.int32, (4 * GATE, 4 * GATE), 1)
    return jnp.where((big_i >> 6) == (big_j >> 6), wide, jnp.zeros_like(wide))


HALF = ROWS // 2
BONDS = CHI // 2
STEP = 512


def put_level(wide, t, value):
    for h in range(2):
        wide[h, pl.ds(t, CHI, stride=LEVELS), :] = value[:, h * 128 : (h + 1) * 128]


def take_slabs(wide, put):
    for h in range(2):
        for u in range(LEVELS // 2):
            pair = [wide[h, pl.ds(2 * u + e, CHI, stride=LEVELS), :] for e in range(2)]
            put(h, u, jnp.concatenate(pair, axis=1).astype(BF16))


def identity(dtype):
    i = lax.broadcasted_iota(jnp.int32, (CHI, CHI), 0)
    j = lax.broadcasted_iota(jnp.int32, (CHI, CHI), 1)
    return jnp.where(i == j, 1.0, 0.0).astype(dtype)


def two_site(lhs_of, weights, y, a0):
    for p in range(2):
        block = lhs_of(p)
        for u in range(LEVELS // 2):
            made = dot(block, weights[p, u * CHI : (u + 1) * CHI, :]).reshape(BONDS, LEVELS, CHI)
            both = jnp.concatenate([made[:, :, :128], made[:, :, 128:]], axis=1).astype(BF16)
            y[pl.ds(a0, BONDS), 16 * u : 16 * u + 16, p * 128 : (p + 1) * 128] = both


def gated(y, gate, m, rows):
    bonds = STEP // LEVELS

    def some(i, _):
        r0 = pl.multiple_of(i * STEP, STEP)
        a0 = pl.multiple_of(i * bonds, bonds)
        for j in range(bonds // 4):
            four = y[pl.ds(a0 + 4 * j, 4)].reshape(4 * GATE, CHI)
            o = dot(gate[...], four).reshape(4, LEVELS, LEVELS, CHI)
            for h in range(2):
                at = pl.multiple_of(r0 + j * 32 + h * 16, 16)
                for t in range(LEVELS):
                    m[pl.ds(at, 16), t * CHI : (t + 1) * CHI] = jnp.concatenate(
                        [o[2 * h, t], o[2 * h + 1, t]], axis=0
                    ).astype(BF16)
        return 0

    lax.fori_loop(0, rows // STEP, some, 0)


def factor(ab, alongside):
    ab[:, CHI:] = identity(F32)
    for o in range(0, CHI, BLOCK):
        e = o + BLOCK
        w = inverse_factor(ab[o:e, o:e])
        alongside(o // BLOCK)
        panel = dot_split(w, ab[o:e, :])
        ab[o:e, CHI:] = panel[:, CHI:]
        if e < CHI:
            ab[e:, :] = ab[e:, :] - dot_split(panel[:, e:CHI], panel, ((0,), (0,)))


LEFT_SCALE = LEVELS**0.5 * CHI**0.25
RIGHT_SCALE = LEFT_SCALE * ROWS**-0.5


def first_kernel(own, recv, sk_own, sk_recv, out_a, out_b, lhs, raw, wts, sk, gate, y, m, s, st, wide, q, ab, sems):
    is_left = lax.rem(lax.axis_index("site"), 2) == 0
    outs = (out_a, out_b)

    def fetch(left, right, sketch):
        return (
            pltpu.make_async_copy(right, raw, sems.at[0]),
            pltpu.make_async_copy(left.at[pl.ds(0, HALF)], lhs.at[0], sems.at[1]),
            pltpu.make_async_copy(left.at[pl.ds(HALF, HALF)], lhs.at[1], sems.at[2]),
            pltpu.make_async_copy(sketch, sk, sems.at[3]),
        )

    copies = fetch(own, recv, sk_own)

    @pl.when(is_left)
    def _():
        for copy in copies:
            copy.start()

    @pl.when(jnp.logical_not(is_left))
    def _():
        for copy in fetch(recv, own, sk_recv):
            copy.start()

    copies[0].wait()
    for h in range(2):
        wide[h] = raw[:, h * 128 : (h + 1) * 128].astype(F32)

    def put(h, u, value):
        wts[h, u * CHI : (u + 1) * CHI, :] = value

    take_slabs(wide, put)
    copies[1].wait()
    copies[2].wait()

    def product(x, _):
        two_site(lambda p: lhs[x], wts, y, pl.multiple_of(x * BONDS, BONDS))
        return 0

    lax.fori_loop(0, 2, product, 0)
    copies[3].wait()
    gate[...] = gate_matrix(sk[ROWS:, :])
    gated(y, gate, m, ROWS)

    def sample(i, _):
        r0 = pl.multiple_of(i * HALF, HALF)
        s[pl.ds(r0, HALF), :] = dot(m[pl.ds(r0, HALF), :], sk[:ROWS, :]).astype(BF16)
        return 0

    lax.fori_loop(0, 2, sample, 0)
    st[...] = dot(identity(BF16), s[...], ((1,), (1,))).astype(BF16)
    ab[:, :CHI] = dot(st[...], s[...])

    def alongside(j):
        for t in (2 * j, 2 * j + 1):
            q[:, t * CHI : (t + 1) * CHI] = dot(st[...], m[:, t * CHI : (t + 1) * CHI]).astype(BF16)

    factor(ab, alongside)

    @pl.when(is_left)
    def _():
        made = dot(s[...], (ab[:, CHI:] * LEFT_SCALE).astype(BF16), ((1,), (1,)))
        for h in range(2):
            wide[h] = made[:, h * 128 : (h + 1) * 128]

        def put_out(h, u, value):
            outs[h][u * CHI : (u + 1) * CHI, :] = value

        take_slabs(wide, put_out)

    @pl.when(jnp.logical_not(is_left))
    def _():
        inv = (ab[:, CHI:] * RIGHT_SCALE).astype(BF16)
        for t in range(LEVELS):
            put_level(wide, t, dot(inv, q[:, t * CHI : (t + 1) * CHI]))
        for x in range(2):
            for h in range(2):
                outs[x][:, h * 128 : (h + 1) * 128] = wide[h, x * HALF : (x + 1) * HALF, :].astype(BF16)


def half_pair(own_a, own_b, recv, sk_own, sk_recv, lhs, wts, sk, gate, y, m, sems, is_left):
    def fetch(left_a, left_b, right_a, right_b, sketch):
        return (
            pltpu.make_async_copy(left_a, lhs.at[0], sems.at[0]),
            pltpu.make_async_copy(left_b, lhs.at[1], sems.at[1]),
            pltpu.make_async_copy(right_a, wts.at[0], sems.at[2]),
            pltpu.make_async_copy(right_b, wts.at[1], sems.at[3]),
            pltpu.make_async_copy(sketch, sk, sems.at[4]),
        )

    copies = fetch(own_a, own_b, recv, recv, sk_own)

    @pl.when(is_left)
    def _():
        for copy in copies:
            copy.start()

    @pl.when(jnp.logical_not(is_left))
    def _():
        for copy in fetch(recv, recv, own_a, own_b, sk_recv):
            copy.start()

    for copy in copies[:4]:
        copy.wait()
    two_site(lambda p: lhs[p], wts, y, 0)
    copies[4].wait()
    gate[...] = gate_matrix(sk[ROWS:, :])
    gated(y, gate, m, HALF)


def column_half(sk, sh, h):
    for t in range(LEVELS):
        at = t * CHI + h * 128
        sh[t * 128 : (t + 1) * 128, :] = sk[at : at + 128, :]


def sampled_rows(m, sh, g):
    lanes = [m[:, t * CHI + g * 128 : t * CHI + (g + 1) * 128] for t in range(LEVELS)]
    return dot(jnp.concatenate(lanes, axis=1), sh[...])


def role():
    me = lax.axis_index("site")
    return lax.rem(me, 2) == 1, (me > 0) & (me < lax.axis_size("site") - 1)


def mid_kernel(own_a, own_b, recv, sk_own, sk_recv, acc, s0, lhs, wts, sk, sh, gate, y, m, sems):
    is_left, busy = role()

    @pl.when(busy)
    def _():
        half_pair(own_a, own_b, recv, sk_own, sk_recv, lhs, wts, sk, gate, y, m, sems, is_left)

        @pl.when(is_left)
        def _():
            column_half(sk, sh, 0)
            for g in range(2):
                acc[g * HALF : (g + 1) * HALF, :] = sampled_rows(m, sh, g)
            s0[...] = jnp.zeros_like(s0)

        @pl.when(jnp.logical_not(is_left))
        def _():
            s0[...] = dot(m[...], sk[:ROWS, :]).astype(BF16)
            turned = dot(identity(BF16), s0[...], ((1,), (1,))).astype(BF16)
            for t in range(LEVELS):
                acc[t * CHI : (t + 1) * CHI, :] = dot(turned, m[:, t * CHI : (t + 1) * CHI])


def last_kernel(
    own_a, own_b, recv, sk_own, sk_recv, acc_in, s0_in, out, lhs, wts, sk, sh, gate, y, m, acc, s, st, wide, q, ab, sems, sems_acc
):
    is_left, busy = role()
    owns = (own_a, own_b)

    @pl.when(busy)
    def _():
        get_acc = pltpu.make_async_copy(acc_in, acc, sems_acc.at[0])
        get_s0 = pltpu.make_async_copy(s0_in, s.at[pl.ds(0, HALF)], sems_acc.at[1])
        get_acc.start()
        get_s0.start()
        half_pair(own_a, own_b, recv, sk_own, sk_recv, lhs, wts, sk, gate, y, m, sems, is_left)
        get_acc.wait()
        get_s0.wait()

        @pl.when(is_left)
        def _():
            column_half(sk, sh, 1)
            for g in range(2):
                rows = slice(g * HALF, (g + 1) * HALF)
                s[rows, :] = (acc[rows, :] + sampled_rows(m, sh, g)).astype(BF16)

        @pl.when(jnp.logical_not(is_left))
        def _():
            s[HALF:, :] = dot(m[...], sk[:ROWS, :]).astype(BF16)

        st[...] = dot(identity(BF16), s[...], ((1,), (1,))).astype(BF16)
        ab[:, :CHI] = dot(st[...], s[...])

        def alongside(j):
            for t in (2 * j, 2 * j + 1):
                more = dot(st[:, HALF:], m[:, t * CHI : (t + 1) * CHI])
                q[:, t * CHI : (t + 1) * CHI] = (acc[t * CHI : (t + 1) * CHI, :] + more).astype(BF16)

        factor(ab, alongside)

        @pl.when(is_left)
        def _():
            out[...] = dot(s[...], (ab[:, CHI:] * LEFT_SCALE).astype(BF16), ((1,), (1,))).astype(BF16)

        @pl.when(jnp.logical_not(is_left))
        def _():
            inv = (ab[:, CHI:] * RIGHT_SCALE).astype(BF16)
            for t in range(LEVELS):
                put_level(wide, t, dot(inv, q[:, t * CHI : (t + 1) * CHI]))
            for h in range(2):
                out[:, h * 128 : (h + 1) * 128] = wide[h].astype(BF16)

    @pl.when(jnp.logical_not(busy))
    def _():
        for x in range(2):
            copy = pltpu.make_async_copy(owns[x], lhs.at[x], sems.at[x])
            copy.start()
            copy.wait()

        @pl.when(is_left)
        def _():
            for x in range(2):
                out[x * HALF : (x + 1) * HALF, :] = lhs[x]

        @pl.when(jnp.logical_not(is_left))
        def _():
            for h in range(2):
                for u in range(LEVELS // 2):
                    for e in range(2):
                        slab = lhs[h, u * CHI : (u + 1) * CHI, e * 128 : (e + 1) * 128].astype(F32)
                        wide[h, pl.ds(2 * u + e, CHI, stride=LEVELS), :] = slab
            for h in range(2):
                out[:, h * 128 : (h + 1) * 128] = wide[h].astype(BF16)


HALF_ARRAY = jax.ShapeDtypeStruct((HALF, CHI), BF16)
HALVES = pltpu.VMEM((2, HALF, CHI), BF16)
WHOLE = pltpu.VMEM((ROWS, CHI), BF16)
TURNED = pltpu.VMEM((CHI, ROWS), BF16)
SKETCH = pltpu.VMEM((ROWS + GATE, CHI), BF16)
GATES = pltpu.VMEM((4 * GATE, 4 * GATE), BF16)
WIDE = pltpu.VMEM((2, ROWS, 128), F32)
GRAM = pltpu.VMEM((CHI, 2 * CHI), F32)


def first_layer(own, recv, sk_own, sk_recv):
    return pl.pallas_call(
        first_kernel,
        out_shape=(HALF_ARRAY, HALF_ARRAY),
        in_specs=[ANY] * 4,
        out_specs=(VMEM, VMEM),
        scratch_shapes=[
            HALVES,
            WHOLE,
            HALVES,
            SKETCH,
            GATES,
            pltpu.VMEM((CHI, GATE, CHI), BF16),
            pltpu.VMEM((ROWS, ROWS), BF16),
            WHOLE,
            TURNED,
            WIDE,
            TURNED,
            GRAM,
            pltpu.SemaphoreType.DMA((4,)),
        ],
        compiler_params=pltpu.CompilerParams(vmem_limit_bytes=32 << 20),
        name="first",
    )(own, recv, sk_own, sk_recv)


HALF_SCRATCH = [
    HALVES,
    HALVES,
    SKETCH,
    pltpu.VMEM((HALF, CHI), BF16),
    GATES,
    pltpu.VMEM((BONDS, GATE, CHI), BF16),
    pltpu.VMEM((HALF, ROWS), BF16),
]


def second_start(own_a, own_b, recv, sk_own, sk_recv):
    return pl.pallas_call(
        mid_kernel,
        out_shape=(jax.ShapeDtypeStruct((ROWS, CHI), F32), HALF_ARRAY),
        in_specs=[ANY] * 5,
        out_specs=(VMEM, VMEM),
        scratch_shapes=[*HALF_SCRATCH, pltpu.SemaphoreType.DMA((5,))],
        compiler_params=pltpu.CompilerParams(vmem_limit_bytes=24 << 20),
        cost_estimate=pl.CostEstimate(flops=5 << 30, bytes_accessed=8 << 20, transcendentals=0),
        name="mid",
    )(own_a, own_b, recv, sk_own, sk_recv)


def second_end(own_a, own_b, recv, sk_own, sk_recv, acc, s0):
    return pl.pallas_call(
        last_kernel,
        out_shape=jax.ShapeDtypeStruct((ROWS, CHI), BF16),
        in_specs=[ANY] * 7,
        out_specs=VMEM,
        scratch_shapes=[
            *HALF_SCRATCH,
            pltpu.VMEM((ROWS, CHI), F32),
            WHOLE,
            TURNED,
            WIDE,
            TURNED,
            GRAM,
            pltpu.SemaphoreType.DMA((5,)),
            pltpu.SemaphoreType.DMA((2,)),
        ],
        compiler_params=pltpu.CompilerParams(vmem_limit_bytes=32 << 20),
        name="last",
    )(own_a, own_b, recv, sk_own, sk_recv, acc, s0)


def pack(sketch, gate):
    return jnp.concatenate([sketch.astype(BF16), jnp.concatenate([gate] * 4, axis=1)], axis=0)


def per_device(site_tensors, first_gates, second_gates, first_sketch, second_sketch):
    devices = lax.axis_size("site")
    inside = [(i, i ^ 1) for i in range(devices)]
    across = [(i, (i + 1) % devices if i % 2 else (i - 1) % devices) for i in range(devices)]
    own = site_tensors[0].reshape(ROWS, CHI)
    recv = lax.ppermute(own, "site", inside)
    sk0 = pack(first_sketch[0], first_gates[0])
    sk0_recv = lax.ppermute(sk0, "site", inside)
    sk1 = pack(second_sketch[0], second_gates[0])
    sk1_recv = lax.ppermute(sk1, "site", across)
    own_a, own_b = first_layer(own, recv, sk0, sk0_recv)
    recv_a = lax.ppermute(own_a, "site", across)
    recv_b = lax.ppermute(own_b, "site", across)
    acc, s0 = second_start(own_a, own_b, recv_a, sk1, sk1_recv)
    made = second_end(own_a, own_b, recv_b, sk1, sk1_recv, acc, s0)
    return made.reshape(1, CHI, LEVELS, CHI)


def solution(mesh):
    in_specs = (
        P("site", None, None, None),
        P("site", None, None),
        P("site", None, None),
        P("site", None, None),
        P("site", None, None),
    )
    out_specs = P("site", None, None, None)
    return jax.shard_map(
        per_device, mesh=mesh, in_specs=in_specs, out_specs=out_specs, check_vma=False
    )
```

```python
import jax
import jax.numpy as jnp
from jax import lax
from jax.experimental import pallas as pl
from jax.experimental.pallas import tpu as pltpu
from jax.sharding import PartitionSpec as P

F32 = jnp.float32
BF16 = jnp.bfloat16
ANY = pl.BlockSpec(memory_space=pl.ANY)
VMEM = pl.BlockSpec(memory_space=pltpu.VMEM)
CHI = 256
LEVELS = 8
ROWS = CHI * LEVELS
GATE = LEVELS * LEVELS
BLOCK = 64


def lanes_of(v, k):
    return jnp.broadcast_to(v[:, k : k + 1], (8, 128))


def row_of(v, r):
    return jnp.broadcast_to(v[r : r + 1, :], (8, 128))


def inverse_factor(diag_block):
    nb = BLOCK
    nv = nb // 8
    rows = lax.broadcasted_iota(jnp.int32, (nb, nb), 0)
    cols = lax.broadcasted_iota(jnp.int32, (nb, nb), 1)
    beside = jnp.concatenate([diag_block, jnp.where(rows == cols, 1.0, 0.0).astype(F32)], axis=1)
    v = [beside[8 * q : 8 * q + 8, :] for q in range(nv)]
    sub = lax.broadcasted_iota(jnp.int32, (8, 128), 0)
    scale = [jnp.ones((8, 128), F32)] * nv
    c = [[lanes_of(v[q], i) for q in range(nv)] for i in range(4)]
    for k in range(0, nb, 4):
        p, r = divmod(k, 8)
        last = k + 4 >= nb
        if not last:
            p2, r2 = divmod(k + 4, 8)
            ahead = [[lanes_of(v[q], k + 4 + i) for q in range(p2, nv)] for i in range(4)]
        row = [row_of(v[p], r + i) for i in range(4)]
        g = [[row_of(c[j][0], r + i) if i >= j else None for j in range(4)] for i in range(4)]
        a, b, d = g[0][0], g[1][0], g[1][1]
        det = a * d - b * b
        idet = 1.0 / det

        def adjugate(x, y):
            return x * d - y * b, y * a - x * b

        n20, n21 = adjugate(g[2][0], g[2][1])
        n30, n31 = adjugate(g[3][0], g[3][1])
        a2 = g[2][2] - (g[2][0] * n20 + g[2][1] * n21) * idet
        b2 = g[3][2] - (g[3][0] * n20 + g[3][1] * n21) * idet
        d2 = g[3][3] - (g[3][0] * n30 + g[3][1] * n31) * idet
        det2 = a2 * d2 - b2 * b2
        idet2 = 1.0 / det2
        m20, m21, m30, m31 = n20 * idet, n21 * idet, n30 * idet, n31 * idet

        def panel_solve(x0, x1, x2, x3):
            u0, u1 = adjugate(x0, x1)
            y2 = x2 - (m20 * x0 + m21 * x1)
            y3 = x3 - (m30 * x0 + m31 * x1)
            return u0 * idet, u1 * idet, (y2 * d2 - y3 * b2) * idet2, (y3 * a2 - y2 * b2) * idet2, y2, y3

        ce = [
            (
                c[0][q - p],
                c[1][q - p],
                c[2][q - p] - (m20 * c[0][q - p] + m21 * c[1][q - p]),
                c[3][q - p] - (m30 * c[0][q - p] + m31 * c[1][q - p]),
            )
            for q in range(p, nv)
        ]
        if not last:
            across = panel_solve(*[c[j][p2 - p] for j in range(4)])[:4]
            c_next = []
            for i in range(4):
                hs = [row_of(x, r2 + i) for x in across]
                c_next.append(
                    [
                        (ahead[i][q - p2] - (ce[q - p][0] * hs[0] + ce[q - p][1] * hs[1]))
                        - (ce[q - p][2] * hs[2] + ce[q - p][3] * hs[3])
                        for q in range(p2, nv)
                    ]
                )
        u0, u1, h2, h3, row2, row3 = panel_solve(*row)
        below = sub > r + 3
        for q in range(p, nv):
            cq = ce[q - p]
            if q == p:
                cq = [jnp.where(below, x, 0.0) for x in cq]
            v[q] = (v[q] - (cq[0] * u0 + cq[1] * u1)) - (cq[2] * h2 + cq[3] * h3)
        ia = 1.0 / a
        ia2 = 1.0 / a2
        row1 = row[1] - (b * ia) * row[0]
        row3 = row3 - (b2 * ia2) * row2
        v[p] = jnp.where(
            sub == r + 1, row1, jnp.where(sub == r + 2, row2, jnp.where(sub == r + 3, row3, v[p]))
        )
        scale[p] = jnp.where(
            sub == r,
            lax.rsqrt(a),
            jnp.where(
                sub == r + 1,
                lax.rsqrt(det * ia),
                jnp.where(sub == r + 2, lax.rsqrt(a2), jnp.where(sub == r + 3, lax.rsqrt(det2 * ia2), scale[p])),
            ),
        )
        if not last:
            c = c_next
    return jnp.concatenate([v[q] * scale[q] for q in range(nv)], axis=0)


def dot(x, y, dims=((1,), (0,))):
    return lax.dot_general(x, y, (dims, ((), ())), preferred_element_type=F32)


def dot_split(x, y, dims=((1,), (0,))):
    xh = x.astype(BF16)
    xl = (x - xh.astype(F32)).astype(BF16)
    yh = y.astype(BF16)
    yl = (y - yh.astype(F32)).astype(BF16)
    return dot(xh, yh, dims) + (dot(xh, yl, dims) + dot(xl, yh, dims))


def gate_matrix(packed):
    i = lax.broadcasted_iota(jnp.int32, (GATE, GATE), 0)
    j = lax.broadcasted_iota(jnp.int32, (GATE, GATE), 1)
    swap = jnp.where(j == (i & 7) * 8 + (i >> 3), 1.0, 0.0).astype(BF16)
    g = dot(dot(swap, packed[:, :GATE]).astype(BF16), swap, ((1,), (1,))).astype(BF16)
    wide = jnp.concatenate([jnp.concatenate([g] * 4, axis=1)] * 4, axis=0)
    big_i = lax.broadcasted_iota(jnp.int32, (4 * GATE, 4 * GATE), 0)
    big_j = lax.broadcasted_iota(jnp.int32, (4 * GATE, 4 * GATE), 1)
    return jnp.where((big_i >> 6) == (big_j >> 6), wide, jnp.zeros_like(wide))


HALF = ROWS // 2
BONDS = CHI // 2
STEP = 512


def put_level(wide, t, value):
    for h in range(2):
        wide[h, pl.ds(t, CHI, stride=LEVELS), :] = value[:, h * 128 : (h + 1) * 128]


def take_slabs(wide, put):
    for h in range(2):
        for u in range(LEVELS // 2):
            pair = [wide[h, pl.ds(2 * u + e, CHI, stride=LEVELS), :] for e in range(2)]
            put(h, u, jnp.concatenate(pair, axis=1).astype(BF16))


def identity(dtype):
    i = lax.broadcasted_iota(jnp.int32, (CHI, CHI), 0)
    j = lax.broadcasted_iota(jnp.int32, (CHI, CHI), 1)
    return jnp.where(i == j, 1.0, 0.0).astype(dtype)


def two_site(lhs_of, weights, y, a0):
    for p in range(2):
        block = lhs_of(p)
        for u in range(LEVELS // 2):
            made = dot(block, weights[p, u * CHI : (u + 1) * CHI, :]).reshape(BONDS, LEVELS, CHI)
            both = jnp.concatenate([made[:, :, :128], made[:, :, 128:]], axis=1).astype(BF16)
            y[pl.ds(a0, BONDS), 16 * u : 16 * u + 16, p * 128 : (p + 1) * 128] = both


def gated(y, gate, m, rows):
    bonds = STEP // LEVELS

    def some(i, _):
        r0 = pl.multiple_of(i * STEP, STEP)
        a0 = pl.multiple_of(i * bonds, bonds)
        for j in range(bonds // 4):
            four = y[pl.ds(a0 + 4 * j, 4)].reshape(4 * GATE, CHI)
            o = dot(gate[...], four).reshape(4, LEVELS, LEVELS, CHI)
            for h in range(2):
                at = pl.multiple_of(r0 + j * 32 + h * 16, 16)
                for t in range(LEVELS):
                    m[pl.ds(at, 16), t * CHI : (t + 1) * CHI] = jnp.concatenate(
                        [o[2 * h, t], o[2 * h + 1, t]], axis=0
                    ).astype(BF16)
        return 0

    lax.fori_loop(0, rows // STEP, some, 0)


def factor(ab, alongside):
    unit = identity(F32)
    gram = ab[:, :CHI]
    largest = jnp.max(gram * unit, keepdims=True)
    ab[:, :CHI] = gram * (1.0 / largest)
    ab[:, CHI:] = unit
    lane = lax.broadcasted_iota(jnp.int32, (BLOCK, 128), 1)
    none = jnp.zeros((BLOCK, 2 * CHI), F32)
    block = ab[:BLOCK, :BLOCK]
    for o in range(0, CHI, BLOCK):
        e = o + BLOCK
        uw = inverse_factor(block)
        alongside(o // BLOCK)
        panel = dot_split(uw, jnp.concatenate([none, ab[o:e, :]], axis=0))
        ab[o:e, CHI:] = panel[:, CHI:]
        if e < CHI:
            tile = o // 128 * 128
            if o == tile:
                w = jnp.concatenate([uw[:, BLOCK:], jnp.zeros((BLOCK, BLOCK), F32)], axis=1)
            else:
                w = jnp.where(lane >= BLOCK, uw, 0.0)
            turned = dot_split(ab[e:, tile : tile + 128], w, ((1,), (1,)))
            top = ab[e : e + BLOCK, :] - dot_split(turned[:BLOCK], panel)
            block = top[:, e : e + BLOCK]
            ab[e : e + BLOCK, :] = top
            if e + BLOCK < CHI:
                ab[e + BLOCK :, :] = ab[e + BLOCK :, :] - dot_split(turned[BLOCK:], panel)
    return lax.rsqrt(largest)


LEFT_SCALE = LEVELS**0.5 * CHI**0.25
RIGHT_SCALE = LEFT_SCALE * ROWS**-0.5


def first_kernel(own, recv, sk_own, sk_recv, out_a, out_b, lhs, raw, wts, sk, gate, y, m, s, st, wide, q, ab, sems):
    is_left = lax.rem(lax.axis_index("site"), 2) == 0
    outs = (out_a, out_b)

    def fetch(left, right, sketch):
        return (
            pltpu.make_async_copy(right, raw, sems.at[0]),
            pltpu.make_async_copy(left.at[pl.ds(0, HALF)], lhs.at[0], sems.at[1]),
            pltpu.make_async_copy(left.at[pl.ds(HALF, HALF)], lhs.at[1], sems.at[2]),
            pltpu.make_async_copy(sketch, sk, sems.at[3]),
        )

    copies = fetch(own, recv, sk_own)

    @pl.when(is_left)
    def _():
        for copy in copies:
            copy.start()

    @pl.when(jnp.logical_not(is_left))
    def _():
        for copy in fetch(recv, own, sk_recv):
            copy.start()

    copies[0].wait()
    for h in range(2):
        wide[h] = raw[:, h * 128 : (h + 1) * 128].astype(F32)

    def put(h, u, value):
        wts[h, u * CHI : (u + 1) * CHI, :] = value

    take_slabs(wide, put)
    copies[1].wait()
    copies[2].wait()

    def product(x, _):
        two_site(lambda p: lhs[x], wts, y, pl.multiple_of(x * BONDS, BONDS))
        return 0

    lax.fori_loop(0, 2, product, 0)
    copies[3].wait()
    gate[...] = gate_matrix(sk[ROWS:, :])
    gated(y, gate, m, ROWS)

    def sample(i, _):
        r0 = pl.multiple_of(i * HALF, HALF)
        s[pl.ds(r0, HALF), :] = dot(m[pl.ds(r0, HALF), :], sk[:ROWS, :]).astype(BF16)
        return 0

    lax.fori_loop(0, 2, sample, 0)
    st[...] = dot(identity(BF16), s[...], ((1,), (1,))).astype(BF16)
    ab[:, :CHI] = dot(st[...], s[...])

    def alongside(j):
        for t in (2 * j, 2 * j + 1):
            q[:, t * CHI : (t + 1) * CHI] = dot(st[...], m[:, t * CHI : (t + 1) * CHI]).astype(BF16)

    unscale = factor(ab, alongside)

    @pl.when(is_left)
    def _():
        made = dot(s[...], (ab[:, CHI:] * (unscale * LEFT_SCALE)).astype(BF16), ((1,), (1,)))
        for h in range(2):
            wide[h] = made[:, h * 128 : (h + 1) * 128]

        def put_out(h, u, value):
            outs[h][u * CHI : (u + 1) * CHI, :] = value

        take_slabs(wide, put_out)

    @pl.when(jnp.logical_not(is_left))
    def _():
        inv = (ab[:, CHI:] * (unscale * RIGHT_SCALE)).astype(BF16)
        for t in range(LEVELS):
            put_level(wide, t, dot(inv, q[:, t * CHI : (t + 1) * CHI]))
        for x in range(2):
            for h in range(2):
                outs[x][:, h * 128 : (h + 1) * 128] = wide[h, x * HALF : (x + 1) * HALF, :].astype(BF16)


def half_pair(own_a, own_b, recv, sk_own, sk_recv, lhs, wts, sk, gate, y, m, sems, is_left):
    def fetch(left_a, left_b, right_a, right_b, sketch):
        return (
            pltpu.make_async_copy(left_a, lhs.at[0], sems.at[0]),
            pltpu.make_async_copy(left_b, lhs.at[1], sems.at[1]),
            pltpu.make_async_copy(right_a, wts.at[0], sems.at[2]),
            pltpu.make_async_copy(right_b, wts.at[1], sems.at[3]),
            pltpu.make_async_copy(sketch, sk, sems.at[4]),
        )

    copies = fetch(own_a, own_b, recv, recv, sk_own)

    @pl.when(is_left)
    def _():
        for copy in copies:
            copy.start()

    @pl.when(jnp.logical_not(is_left))
    def _():
        for copy in fetch(recv, recv, own_a, own_b, sk_recv):
            copy.start()

    for copy in copies[:4]:
        copy.wait()
    two_site(lambda p: lhs[p], wts, y, 0)
    copies[4].wait()
    gate[...] = gate_matrix(sk[ROWS:, :])
    gated(y, gate, m, HALF)


def column_half(sk, sh, h):
    for t in range(LEVELS):
        at = t * CHI + h * 128
        sh[t * 128 : (t + 1) * 128, :] = sk[at : at + 128, :]


def sampled_rows(m, sh, g):
    lanes = [m[:, t * CHI + g * 128 : t * CHI + (g + 1) * 128] for t in range(LEVELS)]
    return dot(jnp.concatenate(lanes, axis=1), sh[...])


def role():
    me = lax.axis_index("site")
    return lax.rem(me, 2) == 1, (me > 0) & (me < lax.axis_size("site") - 1)


def mid_kernel(own_a, own_b, recv, sk_own, sk_recv, acc, s0, m, lhs, wts, sk, sh, gate, y, sems):
    is_left, busy = role()

    @pl.when(busy)
    def _():
        half_pair(own_a, own_b, recv, sk_own, sk_recv, lhs, wts, sk, gate, y, m, sems, is_left)

        @pl.when(is_left)
        def _():
            column_half(sk, sh, 0)
            for g in range(2):
                acc[g * HALF : (g + 1) * HALF, :] = sampled_rows(m, sh, g)
            s0[...] = jnp.zeros_like(s0)

        @pl.when(jnp.logical_not(is_left))
        def _():
            s0[...] = dot(m[...], sk[:ROWS, :]).astype(BF16)


def last_kernel(
    own_a, own_b, recv, sk_own, sk_recv, acc, s0, m0, out, lhs, wts, sk, sh, gate, y, m, s, st, wide, q, ab, sems
):
    is_left, busy = role()
    owns = (own_a, own_b)

    @pl.when(busy)
    def _():
        half_pair(own_a, own_b, recv, sk_own, sk_recv, lhs, wts, sk, gate, y, m, sems, is_left)

        @pl.when(is_left)
        def _():
            column_half(sk, sh, 1)
            for g in range(2):
                rows = slice(g * HALF, (g + 1) * HALF)
                s[rows, :] = (acc[rows, :] + sampled_rows(m, sh, g)).astype(BF16)

        @pl.when(jnp.logical_not(is_left))
        def _():
            s[:HALF, :] = s0[...]
            s[HALF:, :] = dot(m[...], sk[:ROWS, :]).astype(BF16)

        st[...] = dot(identity(BF16), s[...], ((1,), (1,))).astype(BF16)
        ab[:, :CHI] = dot(st[...], s[...])

        def alongside(j):
            for t in (2 * j, 2 * j + 1):
                columns = slice(t * CHI, (t + 1) * CHI)
                made = dot(st[:, :HALF], m0[:, columns]) + dot(st[:, HALF:], m[:, columns])
                q[:, columns] = made.astype(BF16)

        unscale = factor(ab, alongside)

        @pl.when(is_left)
        def _():
            out[...] = dot(s[...], (ab[:, CHI:] * (unscale * LEFT_SCALE)).astype(BF16), ((1,), (1,))).astype(BF16)

        @pl.when(jnp.logical_not(is_left))
        def _():
            inv = (ab[:, CHI:] * (unscale * RIGHT_SCALE)).astype(BF16)
            for t in range(LEVELS):
                put_level(wide, t, dot(inv, q[:, t * CHI : (t + 1) * CHI]))
            for h in range(2):
                out[:, h * 128 : (h + 1) * 128] = wide[h].astype(BF16)

    @pl.when(jnp.logical_not(busy))
    def _():
        for x in range(2):
            copy = pltpu.make_async_copy(owns[x], lhs.at[x], sems.at[x])
            copy.start()
            copy.wait()

        @pl.when(is_left)
        def _():
            for x in range(2):
                out[x * HALF : (x + 1) * HALF, :] = lhs[x]

        @pl.when(jnp.logical_not(is_left))
        def _():
            for h in range(2):
                for u in range(LEVELS // 2):
                    for e in range(2):
                        slab = lhs[h, u * CHI : (u + 1) * CHI, e * 128 : (e + 1) * 128].astype(F32)
                        wide[h, pl.ds(2 * u + e, CHI, stride=LEVELS), :] = slab
            for h in range(2):
                out[:, h * 128 : (h + 1) * 128] = wide[h].astype(BF16)


HALF_ARRAY = jax.ShapeDtypeStruct((HALF, CHI), BF16)
HALVES = pltpu.VMEM((2, HALF, CHI), BF16)
WHOLE = pltpu.VMEM((ROWS, CHI), BF16)
TURNED = pltpu.VMEM((CHI, ROWS), BF16)
SKETCH = pltpu.VMEM((ROWS + GATE, CHI), BF16)
GATES = pltpu.VMEM((4 * GATE, 4 * GATE), BF16)
WIDE = pltpu.VMEM((2, ROWS, 128), F32)
GRAM = pltpu.VMEM((CHI, 2 * CHI), F32)


def first_layer(own, recv, sk_own, sk_recv):
    return pl.pallas_call(
        first_kernel,
        out_shape=(HALF_ARRAY, HALF_ARRAY),
        in_specs=[ANY] * 4,
        out_specs=(VMEM, VMEM),
        scratch_shapes=[
            HALVES,
            WHOLE,
            HALVES,
            SKETCH,
            GATES,
            pltpu.VMEM((CHI, GATE, CHI), BF16),
            pltpu.VMEM((ROWS, ROWS), BF16),
            WHOLE,
            TURNED,
            WIDE,
            TURNED,
            GRAM,
            pltpu.SemaphoreType.DMA((4,)),
        ],
        compiler_params=pltpu.CompilerParams(vmem_limit_bytes=32 << 20),
        name="first",
    )(own, recv, sk_own, sk_recv)


HALF_SCRATCH = [
    HALVES,
    HALVES,
    SKETCH,
    pltpu.VMEM((HALF, CHI), BF16),
    GATES,
    pltpu.VMEM((BONDS, GATE, CHI), BF16),
]


def second_start(own_a, own_b, recv, sk_own, sk_recv):
    return pl.pallas_call(
        mid_kernel,
        out_shape=(
            jax.ShapeDtypeStruct((ROWS, CHI), F32),
            HALF_ARRAY,
            jax.ShapeDtypeStruct((HALF, ROWS), BF16),
        ),
        in_specs=[ANY] * 5,
        out_specs=(VMEM, VMEM, VMEM),
        scratch_shapes=[*HALF_SCRATCH, pltpu.SemaphoreType.DMA((5,))],
        compiler_params=pltpu.CompilerParams(vmem_limit_bytes=24 << 20),
        cost_estimate=pl.CostEstimate(flops=5 << 30, bytes_accessed=8 << 20, transcendentals=0),
        name="mid",
    )(own_a, own_b, recv, sk_own, sk_recv)


def second_end(own_a, own_b, recv, sk_own, sk_recv, acc, s0, m0):
    return pl.pallas_call(
        last_kernel,
        out_shape=jax.ShapeDtypeStruct((ROWS, CHI), BF16),
        in_specs=[*[ANY] * 5, VMEM, VMEM, VMEM],
        out_specs=VMEM,
        scratch_shapes=[
            *HALF_SCRATCH,
            pltpu.VMEM((HALF, ROWS), BF16),
            WHOLE,
            TURNED,
            WIDE,
            TURNED,
            GRAM,
            pltpu.SemaphoreType.DMA((5,)),
        ],
        compiler_params=pltpu.CompilerParams(vmem_limit_bytes=32 << 20),
        name="last",
    )(own_a, own_b, recv, sk_own, sk_recv, acc, s0, m0)


def pack(sketch, gate):
    return jnp.concatenate([sketch.astype(BF16), jnp.concatenate([gate] * 4, axis=1)], axis=0)


def per_device(site_tensors, first_gates, second_gates, first_sketch, second_sketch):
    devices = lax.axis_size("site")
    inside = [(i, i ^ 1) for i in range(devices)]
    across = [(i, (i + 1) % devices if i % 2 else (i - 1) % devices) for i in range(devices)]
    own = site_tensors[0].reshape(ROWS, CHI)
    recv = lax.ppermute(own, "site", inside)
    sk0 = pack(first_sketch[0], first_gates[0])
    sk0_recv = lax.ppermute(sk0, "site", inside)
    sk1 = pack(second_sketch[0], second_gates[0])
    sk1_recv = lax.ppermute(sk1, "site", across)
    own_a, own_b = first_layer(own, recv, sk0, sk0_recv)
    recv_a = lax.ppermute(own_a, "site", across)
    recv_b = lax.ppermute(own_b, "site", across)
    acc, s0, m0 = second_start(own_a, own_b, recv_a, sk1, sk1_recv)
    made = second_end(own_a, own_b, recv_b, sk1, sk1_recv, acc, s0, m0)
    return made.reshape(1, CHI, LEVELS, CHI)


def solution(mesh):
    in_specs = (
        P("site", None, None, None),
        P("site", None, None),
        P("site", None, None),
        P("site", None, None),
        P("site", None, None),
    )
    out_specs = P("site", None, None, None)
    return jax.shard_map(
        per_device, mesh=mesh, in_specs=in_specs, out_specs=out_specs, check_vma=False
    )
```

```python
import jax
import jax.numpy as jnp
from jax import lax
from jax.experimental import pallas as pl
from jax.experimental.pallas import tpu as pltpu
from jax.sharding import PartitionSpec as P

F32 = jnp.float32
BF16 = jnp.bfloat16
VMEM = pl.BlockSpec(memory_space=pltpu.VMEM)
CHI = 256
LEVELS = 8
ROWS = CHI * LEVELS
GATE = LEVELS * LEVELS
BLOCK = 64


def lanes_of(v, k):
    return jnp.broadcast_to(v[:, k : k + 1], (8, 128))


def row_of(v, r):
    return jnp.broadcast_to(v[r : r + 1, :], (8, 128))


def inverse_factor(diag_block):
    nb = BLOCK
    nv = nb // 8
    rows = lax.broadcasted_iota(jnp.int32, (nb, nb), 0)
    cols = lax.broadcasted_iota(jnp.int32, (nb, nb), 1)
    beside = jnp.concatenate([diag_block, jnp.where(rows == cols, 1.0, 0.0).astype(F32)], axis=1)
    v = [beside[8 * q : 8 * q + 8, :] for q in range(nv)]
    sub = lax.broadcasted_iota(jnp.int32, (8, 128), 0)
    scale = [jnp.ones((8, 128), F32)] * nv
    c = [[lanes_of(v[q], i) for q in range(nv)] for i in range(4)]
    for k in range(0, nb, 4):
        p, r = divmod(k, 8)
        last = k + 4 >= nb
        if not last:
            p2, r2 = divmod(k + 4, 8)
            ahead = [[lanes_of(v[q], k + 4 + i) for q in range(p2, nv)] for i in range(4)]
        row = [row_of(v[p], r + i) for i in range(4)]
        g = [[row_of(c[j][0], r + i) if i >= j else None for j in range(4)] for i in range(4)]
        a, b, d = g[0][0], g[1][0], g[1][1]
        det = a * d - b * b
        idet = 1.0 / det

        def adjugate(x, y):
            return x * d - y * b, y * a - x * b

        n20, n21 = adjugate(g[2][0], g[2][1])
        n30, n31 = adjugate(g[3][0], g[3][1])
        a2 = g[2][2] - (g[2][0] * n20 + g[2][1] * n21) * idet
        b2 = g[3][2] - (g[3][0] * n20 + g[3][1] * n21) * idet
        d2 = g[3][3] - (g[3][0] * n30 + g[3][1] * n31) * idet
        det2 = a2 * d2 - b2 * b2
        idet2 = 1.0 / det2
        m20, m21, m30, m31 = n20 * idet, n21 * idet, n30 * idet, n31 * idet

        def panel_solve(x0, x1, x2, x3):
            u0, u1 = adjugate(x0, x1)
            y2 = x2 - (m20 * x0 + m21 * x1)
            y3 = x3 - (m30 * x0 + m31 * x1)
            return u0 * idet, u1 * idet, (y2 * d2 - y3 * b2) * idet2, (y3 * a2 - y2 * b2) * idet2, y2, y3

        ce = [
            (
                c[0][q - p],
                c[1][q - p],
                c[2][q - p] - (m20 * c[0][q - p] + m21 * c[1][q - p]),
                c[3][q - p] - (m30 * c[0][q - p] + m31 * c[1][q - p]),
            )
            for q in range(p, nv)
        ]
        if not last:
            across = panel_solve(*[c[j][p2 - p] for j in range(4)])[:4]
            c_next = []
            for i in range(4):
                hs = [row_of(x, r2 + i) for x in across]
                c_next.append(
                    [
                        (ahead[i][q - p2] - (ce[q - p][0] * hs[0] + ce[q - p][1] * hs[1]))
                        - (ce[q - p][2] * hs[2] + ce[q - p][3] * hs[3])
                        for q in range(p2, nv)
                    ]
                )
        u0, u1, h2, h3, row2, row3 = panel_solve(*row)
        below = sub > r + 3
        for q in range(p, nv):
            cq = ce[q - p]
            if q == p:
                cq = [jnp.where(below, x, 0.0) for x in cq]
            v[q] = (v[q] - (cq[0] * u0 + cq[1] * u1)) - (cq[2] * h2 + cq[3] * h3)
        ia = 1.0 / a
        ia2 = 1.0 / a2
        row1 = row[1] - (b * ia) * row[0]
        row3 = row3 - (b2 * ia2) * row2
        v[p] = jnp.where(
            sub == r + 1, row1, jnp.where(sub == r + 2, row2, jnp.where(sub == r + 3, row3, v[p]))
        )
        scale[p] = jnp.where(
            sub == r,
            lax.rsqrt(a),
            jnp.where(
                sub == r + 1,
                lax.rsqrt(det * ia),
                jnp.where(sub == r + 2, lax.rsqrt(a2), jnp.where(sub == r + 3, lax.rsqrt(det2 * ia2), scale[p])),
            ),
        )
        if not last:
            c = c_next
    return jnp.concatenate([v[q] * scale[q] for q in range(nv)], axis=0)


def dot(x, y, dims=((1,), (0,))):
    return lax.dot_general(x, y, (dims, ((), ())), preferred_element_type=F32)


def dot_split(x, y, dims=((1,), (0,))):
    xh = x.astype(BF16)
    xl = (x - xh.astype(F32)).astype(BF16)
    yh = y.astype(BF16)
    yl = (y - yh.astype(F32)).astype(BF16)
    return dot(xh, yh, dims) + (dot(xh, yl, dims) + dot(xl, yh, dims))


def gate_matrix(packed):
    i = lax.broadcasted_iota(jnp.int32, (GATE, GATE), 0)
    j = lax.broadcasted_iota(jnp.int32, (GATE, GATE), 1)
    swap = jnp.where(j == (i & 7) * 8 + (i >> 3), 1.0, 0.0).astype(BF16)
    g = dot(dot(swap, packed[:, :GATE]).astype(BF16), swap, ((1,), (1,))).astype(BF16)
    wide = jnp.concatenate([jnp.concatenate([g] * 4, axis=1)] * 4, axis=0)
    big_i = lax.broadcasted_iota(jnp.int32, (4 * GATE, 4 * GATE), 0)
    big_j = lax.broadcasted_iota(jnp.int32, (4 * GATE, 4 * GATE), 1)
    return jnp.where((big_i >> 6) == (big_j >> 6), wide, jnp.zeros_like(wide))


HALF = ROWS // 2
BONDS = CHI // 2
STEP = 512


def put_level(wide, t, value):
    for h in range(2):
        wide[h, pl.ds(t, CHI, stride=LEVELS), :] = value[:, h * 128 : (h + 1) * 128]


def take_slabs(wide, put):
    for h in range(2):
        for u in range(LEVELS // 2):
            pair = [wide[h, pl.ds(2 * u + e, CHI, stride=LEVELS), :] for e in range(2)]
            put(h, u, jnp.concatenate(pair, axis=1).astype(BF16))


def identity(dtype):
    i = lax.broadcasted_iota(jnp.int32, (CHI, CHI), 0)
    j = lax.broadcasted_iota(jnp.int32, (CHI, CHI), 1)
    return jnp.where(i == j, 1.0, 0.0).astype(dtype)


def two_site(lhs_of, weights_of, y, a0):
    for p in range(2):
        block, weights = lhs_of(p), weights_of(p)
        for u in range(LEVELS // 2):
            made = dot(block, weights[u * CHI : (u + 1) * CHI, :]).reshape(BONDS, LEVELS, CHI)
            both = jnp.concatenate([made[:, :, :128], made[:, :, 128:]], axis=1).astype(BF16)
            y[pl.ds(a0, BONDS), 16 * u : 16 * u + 16, p * 128 : (p + 1) * 128] = both


def gated(y, gate, m, rows):
    bonds = STEP // LEVELS

    def some(i, _):
        r0 = pl.multiple_of(i * STEP, STEP)
        a0 = pl.multiple_of(i * bonds, bonds)
        for j in range(bonds // 4):
            four = y[pl.ds(a0 + 4 * j, 4)].reshape(4 * GATE, CHI)
            o = dot(gate[...], four).reshape(4, LEVELS, LEVELS, CHI)
            for h in range(2):
                at = pl.multiple_of(r0 + j * 32 + h * 16, 16)
                for t in range(LEVELS):
                    m[pl.ds(at, 16), t * CHI : (t + 1) * CHI] = jnp.concatenate(
                        [o[2 * h, t], o[2 * h + 1, t]], axis=0
                    ).astype(BF16)
        return 0

    lax.fori_loop(0, rows // STEP, some, 0)


def factor(ab, alongside):
    unit = identity(F32)
    gram = ab[:, :CHI]
    largest = jnp.max(gram * unit, keepdims=True)
    ab[:, :CHI] = gram * (1.0 / largest)
    ab[:, CHI:] = unit
    lane = lax.broadcasted_iota(jnp.int32, (BLOCK, 128), 1)
    none = jnp.zeros((BLOCK, 2 * CHI), F32)
    block = ab[:BLOCK, :BLOCK]
    for o in range(0, CHI, BLOCK):
        e = o + BLOCK
        uw = inverse_factor(block)
        alongside(o // BLOCK)
        panel = dot_split(uw, jnp.concatenate([none, ab[o:e, :]], axis=0))
        ab[o:e, CHI:] = panel[:, CHI:]
        if e < CHI:
            tile = o // 128 * 128
            if o == tile:
                w = jnp.concatenate([uw[:, BLOCK:], jnp.zeros((BLOCK, BLOCK), F32)], axis=1)
            else:
                w = jnp.where(lane >= BLOCK, uw, 0.0)
            turned = dot_split(ab[e:, tile : tile + 128], w, ((1,), (1,)))
            top = ab[e : e + BLOCK, :] - dot_split(turned[:BLOCK], panel)
            block = top[:, e : e + BLOCK]
            ab[e : e + BLOCK, :] = top
            if e + BLOCK < CHI:
                ab[e + BLOCK :, :] = ab[e + BLOCK :, :] - dot_split(turned[BLOCK:], panel)
    return lax.rsqrt(largest)


LEFT_SCALE = LEVELS**0.5 * CHI**0.25
RIGHT_SCALE = LEFT_SCALE * ROWS**-0.5


def product_kernel(own, recv, gate_own, gate_recv, m, wts, gate, y, wide):
    is_left = lax.rem(lax.axis_index("site"), 2) == 0

    def product(left, right, small):
        gate[...] = gate_matrix(small[...])
        for h in range(2):
            wide[h] = right[:, h * 128 : (h + 1) * 128].astype(F32)

        def put(h, u, value):
            wts[h, u * CHI : (u + 1) * CHI, :] = value

        take_slabs(wide, put)

        def some(x, _):
            block = left[pl.ds(pl.multiple_of(x * HALF, HALF), HALF), :]
            two_site(lambda p: block, lambda p: wts.at[p], y, pl.multiple_of(x * BONDS, BONDS))
            return 0

        lax.fori_loop(0, 2, some, 0)

    @pl.when(is_left)
    def _():
        product(own, recv, gate_own)

    @pl.when(jnp.logical_not(is_left))
    def _():
        product(recv, own, gate_recv)

    gated(y, gate, m, ROWS)


def first_kernel(m, sk_own, sk_recv, out_a, out_b, s, st, wide, q, ab):
    is_left = lax.rem(lax.axis_index("site"), 2) == 0
    outs = (out_a, out_b)

    def sample(sketch):
        def some(i, _):
            rows = pl.ds(pl.multiple_of(i * HALF, HALF), HALF)
            s[rows, :] = dot(m[rows, :], sketch[:ROWS, :]).astype(BF16)
            return 0

        lax.fori_loop(0, 2, some, 0)

    @pl.when(is_left)
    def _():
        sample(sk_own)

    @pl.when(jnp.logical_not(is_left))
    def _():
        sample(sk_recv)

    st[...] = dot(identity(BF16), s[...], ((1,), (1,))).astype(BF16)
    ab[:, :CHI] = dot(st[...], s[...])

    def alongside(j):
        for t in (2 * j, 2 * j + 1):
            q[:, t * CHI : (t + 1) * CHI] = dot(st[...], m[:, t * CHI : (t + 1) * CHI]).astype(BF16)

    unscale = factor(ab, alongside)

    @pl.when(is_left)
    def _():
        made = dot(s[...], (ab[:, CHI:] * (unscale * LEFT_SCALE)).astype(BF16), ((1,), (1,)))
        for h in range(2):
            wide[h] = made[:, h * 128 : (h + 1) * 128]

        def put_out(h, u, value):
            outs[h][u * CHI : (u + 1) * CHI, :] = value

        take_slabs(wide, put_out)

    @pl.when(jnp.logical_not(is_left))
    def _():
        inv = (ab[:, CHI:] * (unscale * RIGHT_SCALE)).astype(BF16)
        for t in range(LEVELS):
            put_level(wide, t, dot(inv, q[:, t * CHI : (t + 1) * CHI]))
        for x in range(2):
            for h in range(2):
                outs[x][:, h * 128 : (h + 1) * 128] = wide[h, x * HALF : (x + 1) * HALF, :].astype(BF16)


def ready_kernel(sk_own, sk_recv, sk, gate):
    is_left, _ = role()

    def take(packed):
        sk[...] = packed[:ROWS, :]
        gate[...] = gate_matrix(packed[ROWS:, :])

    @pl.when(is_left)
    def _():
        take(sk_own)

    @pl.when(jnp.logical_not(is_left))
    def _():
        take(sk_recv)


def half_pair(own_a, own_b, recv, gate, y, m, is_left):
    owns = (own_a, own_b)

    @pl.when(is_left)
    def _():
        two_site(lambda p: owns[p][...], lambda p: recv, y, 0)

    @pl.when(jnp.logical_not(is_left))
    def _():
        block = recv[...]
        two_site(lambda p: block, lambda p: owns[p], y, 0)

    gated(y, gate, m, HALF)


def column_half(sk, sh, h):
    for t in range(LEVELS):
        at = t * CHI + h * 128
        sh[t * 128 : (t + 1) * 128, :] = sk[at : at + 128, :]


def sampled_rows(m, sh, g):
    lanes = [m[:, t * CHI + g * 128 : t * CHI + (g + 1) * 128] for t in range(LEVELS)]
    return dot(jnp.concatenate(lanes, axis=1), sh[...])


def role():
    me = lax.axis_index("site")
    return lax.rem(me, 2) == 1, (me > 0) & (me < lax.axis_size("site") - 1)


def mid_kernel(own_a, own_b, recv, sk, gate, acc, s0, m, sh, y):
    is_left, busy = role()

    @pl.when(busy)
    def _():
        half_pair(own_a, own_b, recv, gate, y, m, is_left)

        @pl.when(is_left)
        def _():
            column_half(sk, sh, 0)
            for g in range(2):
                acc[g * HALF : (g + 1) * HALF, :] = sampled_rows(m, sh, g)
            s0[...] = jnp.zeros_like(s0)

        @pl.when(jnp.logical_not(is_left))
        def _():
            s0[...] = dot(m[...], sk[...]).astype(BF16)


def last_kernel(
    own_a, own_b, recv, sk, gate, acc, s0, m0, out, sh, y, m, s, st, wide, q, ab
):
    is_left, busy = role()
    owns = (own_a, own_b)

    @pl.when(busy)
    def _():
        half_pair(own_a, own_b, recv, gate, y, m, is_left)

        @pl.when(is_left)
        def _():
            column_half(sk, sh, 1)
            for g in range(2):
                rows = slice(g * HALF, (g + 1) * HALF)
                s[rows, :] = (acc[rows, :] + sampled_rows(m, sh, g)).astype(BF16)

        @pl.when(jnp.logical_not(is_left))
        def _():
            s[:HALF, :] = s0[...]
            s[HALF:, :] = dot(m[...], sk[...]).astype(BF16)

        st[...] = dot(identity(BF16), s[...], ((1,), (1,))).astype(BF16)
        ab[:, :CHI] = dot(st[...], s[...])

        def alongside(j):
            for t in (2 * j, 2 * j + 1):
                columns = slice(t * CHI, (t + 1) * CHI)
                made = dot(st[:, :HALF], m0[:, columns]) + dot(st[:, HALF:], m[:, columns])
                q[:, columns] = made.astype(BF16)

        unscale = factor(ab, alongside)

        @pl.when(is_left)
        def _():
            out[...] = dot(s[...], (ab[:, CHI:] * (unscale * LEFT_SCALE)).astype(BF16), ((1,), (1,))).astype(BF16)

        @pl.when(jnp.logical_not(is_left))
        def _():
            inv = (ab[:, CHI:] * (unscale * RIGHT_SCALE)).astype(BF16)
            for t in range(LEVELS):
                put_level(wide, t, dot(inv, q[:, t * CHI : (t + 1) * CHI]))
            for h in range(2):
                out[:, h * 128 : (h + 1) * 128] = wide[h].astype(BF16)

    @pl.when(jnp.logical_not(busy))
    def _():
        @pl.when(is_left)
        def _():
            for x in range(2):
                out[x * HALF : (x + 1) * HALF, :] = owns[x][...]

        @pl.when(jnp.logical_not(is_left))
        def _():
            for h in range(2):
                for u in range(LEVELS // 2):
                    for e in range(2):
                        slab = owns[h][u * CHI : (u + 1) * CHI, e * 128 : (e + 1) * 128].astype(F32)
                        wide[h, pl.ds(2 * u + e, CHI, stride=LEVELS), :] = slab
            for h in range(2):
                out[:, h * 128 : (h + 1) * 128] = wide[h].astype(BF16)


HALF_ARRAY = jax.ShapeDtypeStruct((HALF, CHI), BF16)
WHOLE = pltpu.VMEM((ROWS, CHI), BF16)
TURNED = pltpu.VMEM((CHI, ROWS), BF16)
WIDE = pltpu.VMEM((2, ROWS, 128), F32)
GRAM = pltpu.VMEM((CHI, 2 * CHI), F32)
FACTOR = [WHOLE, TURNED, WIDE, TURNED, GRAM]
HALF_SCRATCH = [pltpu.VMEM((HALF, CHI), BF16), pltpu.VMEM((BONDS, GATE, CHI), BF16)]


def call(kernel, name, out_shape, scratch, limit, *args):
    single = not isinstance(out_shape, tuple)
    return pl.pallas_call(
        kernel,
        out_shape=out_shape,
        in_specs=[VMEM] * len(args),
        out_specs=VMEM if single else tuple(VMEM for _ in out_shape),
        scratch_shapes=scratch,
        compiler_params=pltpu.CompilerParams(vmem_limit_bytes=limit << 20),
        name=name,
    )(*args)


def pack(sketch, gate):
    return jnp.concatenate([sketch.astype(BF16), jnp.concatenate([gate] * 4, axis=1)], axis=0)


def per_device(site_tensors, first_gates, second_gates, first_sketch, second_sketch):
    devices = lax.axis_size("site")
    inside = [(i, i ^ 1) for i in range(devices)]
    across = [(i, (i + 1) % devices if i % 2 else (i - 1) % devices) for i in range(devices)]
    own = site_tensors[0].reshape(ROWS, CHI)
    recv = lax.ppermute(own, "site", inside)
    gate_recv = lax.ppermute(first_gates[0], "site", inside)
    sk0 = first_sketch[0].astype(BF16)
    sk0_recv = lax.ppermute(sk0, "site", inside)
    sk1 = pack(second_sketch[0], second_gates[0])
    sk1, gate_recv = lax.optimization_barrier((sk1, gate_recv))
    sk1_recv = lax.ppermute(sk1, "site", across)
    product_scratch = [
        pltpu.VMEM((2, HALF, CHI), BF16),
        pltpu.VMEM((4 * GATE, 4 * GATE), BF16),
        pltpu.VMEM((CHI, GATE, CHI), BF16),
        WIDE,
    ]
    whole_matrix = jax.ShapeDtypeStruct((ROWS, ROWS), BF16)
    half_matrix = jax.ShapeDtypeStruct((HALF, ROWS), BF16)
    whole_array = jax.ShapeDtypeStruct((ROWS, CHI), BF16)
    partial = jax.ShapeDtypeStruct((ROWS, CHI), F32)
    gate_shape = jax.ShapeDtypeStruct((4 * GATE, 4 * GATE), BF16)
    m = call(product_kernel, "product", whole_matrix, product_scratch, 24, own, recv, first_gates[0], gate_recv)
    own_a, own_b = call(first_kernel, "first", (HALF_ARRAY, HALF_ARRAY), FACTOR, 24, m, sk0, sk0_recv)
    recv_a = lax.ppermute(own_a, "site", across)
    recv_b = lax.ppermute(own_b, "site", across)
    sk, gate = call(ready_kernel, "ready", (whole_array, gate_shape), [], 8, sk1, sk1_recv)
    acc, s0, m0 = call(
        mid_kernel, "mid", (partial, HALF_ARRAY, half_matrix), HALF_SCRATCH, 24, own_a, own_b, recv_a, sk, gate
    )
    last_scratch = [*HALF_SCRATCH, pltpu.VMEM((HALF, ROWS), BF16), *FACTOR]
    made = call(
        last_kernel, "last", whole_array, last_scratch, 32, own_a, own_b, recv_b, sk, gate, acc, s0, m0
    )
    return made.reshape(1, CHI, LEVELS, CHI)


def solution(mesh):
    in_specs = (
        P("site", None, None, None),
        P("site", None, None),
        P("site", None, None),
        P("site", None, None),
        P("site", None, None),
    )
    out_specs = P("site", None, None, None)
    return jax.shard_map(
        per_device, mesh=mesh, in_specs=in_specs, out_specs=out_specs, check_vma=False
    )
```

```python
import jax
import jax.numpy as jnp
from jax import lax
from jax.experimental import pallas as pl
from jax.experimental.pallas import tpu as pltpu
from jax.sharding import PartitionSpec as P

F32 = jnp.float32
BF16 = jnp.bfloat16
VMEM = pl.BlockSpec(memory_space=pltpu.VMEM)
CHI = 256
LEVELS = 8
ROWS = CHI * LEVELS
GATE = LEVELS * LEVELS
BLOCK = 64


def lanes_of(v, k):
    return jnp.broadcast_to(v[:, k : k + 1], (8, 128))


def row_of(v, r):
    return jnp.broadcast_to(v[r : r + 1, :], (8, 128))


def inverse_factor(diag_block):
    nb = BLOCK
    nv = nb // 8
    rows = lax.broadcasted_iota(jnp.int32, (nb, nb), 0)
    cols = lax.broadcasted_iota(jnp.int32, (nb, nb), 1)
    beside = jnp.concatenate([diag_block, jnp.where(rows == cols, 1.0, 0.0).astype(F32)], axis=1)
    v = [beside[8 * q : 8 * q + 8, :] for q in range(nv)]
    sub = lax.broadcasted_iota(jnp.int32, (8, 128), 0)
    scale = [jnp.ones((8, 128), F32)] * nv
    c = [[lanes_of(v[q], i) for q in range(nv)] for i in range(4)]
    for k in range(0, nb, 4):
        p, r = divmod(k, 8)
        last = k + 4 >= nb
        if not last:
            p2, r2 = divmod(k + 4, 8)
            ahead = [[lanes_of(v[q], k + 4 + i) for q in range(p2, nv)] for i in range(4)]
        row = [row_of(v[p], r + i) for i in range(4)]
        g = [[row_of(c[j][0], r + i) if i >= j else None for j in range(4)] for i in range(4)]
        a, b, d = g[0][0], g[1][0], g[1][1]
        det = a * d - b * b
        idet = 1.0 / det

        def adjugate(x, y):
            return x * d - y * b, y * a - x * b

        n20, n21 = adjugate(g[2][0], g[2][1])
        n30, n31 = adjugate(g[3][0], g[3][1])
        a2 = g[2][2] - (g[2][0] * n20 + g[2][1] * n21) * idet
        b2 = g[3][2] - (g[3][0] * n20 + g[3][1] * n21) * idet
        d2 = g[3][3] - (g[3][0] * n30 + g[3][1] * n31) * idet
        det2 = a2 * d2 - b2 * b2
        idet2 = 1.0 / det2
        m20, m21, m30, m31 = n20 * idet, n21 * idet, n30 * idet, n31 * idet

        def panel_solve(x0, x1, x2, x3):
            u0, u1 = adjugate(x0, x1)
            y2 = x2 - (m20 * x0 + m21 * x1)
            y3 = x3 - (m30 * x0 + m31 * x1)
            return u0 * idet, u1 * idet, (y2 * d2 - y3 * b2) * idet2, (y3 * a2 - y2 * b2) * idet2, y2, y3

        ce = [
            (
                c[0][q - p],
                c[1][q - p],
                c[2][q - p] - (m20 * c[0][q - p] + m21 * c[1][q - p]),
                c[3][q - p] - (m30 * c[0][q - p] + m31 * c[1][q - p]),
            )
            for q in range(p, nv)
        ]
        if not last:
            across = panel_solve(*[c[j][p2 - p] for j in range(4)])[:4]
            c_next = []
            for i in range(4):
                hs = [row_of(x, r2 + i) for x in across]
                c_next.append(
                    [
                        (ahead[i][q - p2] - (ce[q - p][0] * hs[0] + ce[q - p][1] * hs[1]))
                        - (ce[q - p][2] * hs[2] + ce[q - p][3] * hs[3])
                        for q in range(p2, nv)
                    ]
                )
        u0, u1, h2, h3, row2, row3 = panel_solve(*row)
        below = sub > r + 3
        for q in range(p, nv):
            cq = ce[q - p]
            if q == p:
                cq = [jnp.where(below, x, 0.0) for x in cq]
            v[q] = (v[q] - (cq[0] * u0 + cq[1] * u1)) - (cq[2] * h2 + cq[3] * h3)
        ia = 1.0 / a
        ia2 = 1.0 / a2
        row1 = row[1] - (b * ia) * row[0]
        row3 = row3 - (b2 * ia2) * row2
        v[p] = jnp.where(
            sub == r + 1, row1, jnp.where(sub == r + 2, row2, jnp.where(sub == r + 3, row3, v[p]))
        )
        scale[p] = jnp.where(
            sub == r,
            lax.rsqrt(a),
            jnp.where(
                sub == r + 1,
                lax.rsqrt(det * ia),
                jnp.where(sub == r + 2, lax.rsqrt(a2), jnp.where(sub == r + 3, lax.rsqrt(det2 * ia2), scale[p])),
            ),
        )
        if not last:
            c = c_next
    return jnp.concatenate([v[q] * scale[q] for q in range(nv)], axis=0)


def dot(x, y, dims=((1,), (0,))):
    return lax.dot_general(x, y, (dims, ((), ())), preferred_element_type=F32)


def dot_split(x, y, dims=((1,), (0,))):
    xh = x.astype(BF16)
    xl = (x - xh.astype(F32)).astype(BF16)
    yh = y.astype(BF16)
    yl = (y - yh.astype(F32)).astype(BF16)
    return dot(xh, yh, dims) + (dot(xh, yl, dims) + dot(xl, yh, dims))


def gate_matrix(packed):
    i = lax.broadcasted_iota(jnp.int32, (GATE, GATE), 0)
    j = lax.broadcasted_iota(jnp.int32, (GATE, GATE), 1)
    swap = jnp.where(j == (i & 7) * 8 + (i >> 3), 1.0, 0.0).astype(BF16)
    g = dot(dot(swap, packed[:, :GATE]).astype(BF16), swap, ((1,), (1,))).astype(BF16)
    wide = jnp.concatenate([jnp.concatenate([g] * 4, axis=1)] * 4, axis=0)
    big_i = lax.broadcasted_iota(jnp.int32, (4 * GATE, 4 * GATE), 0)
    big_j = lax.broadcasted_iota(jnp.int32, (4 * GATE, 4 * GATE), 1)
    return jnp.where((big_i >> 6) == (big_j >> 6), wide, jnp.zeros_like(wide))


HALF = ROWS // 2
ROW_SITES = 8
BONDS = CHI // 2
STEP = 512


def put_level(wide, t, value):
    for h in range(2):
        wide[h, pl.ds(t, CHI, stride=LEVELS), :] = value[:, h * 128 : (h + 1) * 128]


def take_slabs(wide, put):
    for h in range(2):
        for u in range(LEVELS // 2):
            pair = [wide[h, pl.ds(2 * u + e, CHI, stride=LEVELS), :] for e in range(2)]
            put(h, u, jnp.concatenate(pair, axis=1).astype(BF16))


def identity(dtype):
    i = lax.broadcasted_iota(jnp.int32, (CHI, CHI), 0)
    j = lax.broadcasted_iota(jnp.int32, (CHI, CHI), 1)
    return jnp.where(i == j, 1.0, 0.0).astype(dtype)


def two_site(lhs_of, weights_of, y, a0):
    for p in range(2):
        block, weights = lhs_of(p), weights_of(p)
        for u in range(LEVELS // 2):
            made = dot(block, weights[u * CHI : (u + 1) * CHI, :]).reshape(BONDS, LEVELS, CHI)
            both = jnp.concatenate([made[:, :, :128], made[:, :, 128:]], axis=1).astype(BF16)
            y[pl.ds(a0, BONDS), 16 * u : 16 * u + 16, p * 128 : (p + 1) * 128] = both


def gated(y, gate, m, rows):
    bonds = STEP // LEVELS

    def some(i, _):
        r0 = pl.multiple_of(i * STEP, STEP)
        a0 = pl.multiple_of(i * bonds, bonds)
        for j in range(bonds // 4):
            four = y[pl.ds(a0 + 4 * j, 4)].reshape(4 * GATE, CHI)
            o = dot(gate[...], four).reshape(4, LEVELS, LEVELS, CHI)
            for h in range(2):
                at = pl.multiple_of(r0 + j * 32 + h * 16, 16)
                for t in range(LEVELS):
                    m[pl.ds(at, 16), t * CHI : (t + 1) * CHI] = jnp.concatenate(
                        [o[2 * h, t], o[2 * h + 1, t]], axis=0
                    ).astype(BF16)
        return 0

    lax.fori_loop(0, rows // STEP, some, 0)


def factor(ab, alongside):
    unit = identity(F32)
    gram = ab[:, :CHI]
    largest = jnp.max(gram * unit, keepdims=True)
    ab[:, :CHI] = gram * (1.0 / largest)
    ab[:, CHI:] = unit
    lane = lax.broadcasted_iota(jnp.int32, (BLOCK, 128), 1)
    none = jnp.zeros((BLOCK, 2 * CHI), F32)
    block = ab[:BLOCK, :BLOCK]
    for o in range(0, CHI, BLOCK):
        e = o + BLOCK
        uw = inverse_factor(block)
        alongside(o // BLOCK)
        panel = dot_split(uw, jnp.concatenate([none, ab[o:e, :]], axis=0))
        ab[o:e, CHI:] = panel[:, CHI:]
        if e < CHI:
            tile = o // 128 * 128
            if o == tile:
                w = jnp.concatenate([uw[:, BLOCK:], jnp.zeros((BLOCK, BLOCK), F32)], axis=1)
            else:
                w = jnp.where(lane >= BLOCK, uw, 0.0)
            turned = dot_split(ab[e:, tile : tile + 128], w, ((1,), (1,)))
            top = ab[e : e + BLOCK, :] - dot_split(turned[:BLOCK], panel)
            block = top[:, e : e + BLOCK]
            ab[e : e + BLOCK, :] = top
            if e + BLOCK < CHI:
                ab[e + BLOCK :, :] = ab[e + BLOCK :, :] - dot_split(turned[BLOCK:], panel)
    return lax.rsqrt(largest)


LEFT_SCALE = LEVELS**0.5 * CHI**0.25
RIGHT_SCALE = LEFT_SCALE * ROWS**-0.5


def waits_long():
    return lax.rem(lax.axis_index("site"), ROW_SITES) == 0


def product(left, right, small, m, wts, gate, y, wide):
    gate[...] = gate_matrix(small[...])
    for h in range(2):
        wide[h] = right[:, h * 128 : (h + 1) * 128].astype(F32)

    def put(h, u, value):
        wts[h, u * CHI : (u + 1) * CHI, :] = value

    take_slabs(wide, put)

    def some(x, _):
        block = left[pl.ds(pl.multiple_of(x * HALF, HALF), HALF), :]
        two_site(lambda p: block, lambda p: wts.at[p], y, pl.multiple_of(x * BONDS, BONDS))
        return 0

    lax.fori_loop(0, 2, some, 0)


def early_kernel(own, recv, gate_own, gate_recv, gate_next, m, gate_rows, wts, gate, y, wide):
    gate_rows[...] = jnp.concatenate([gate_next[...]] * 4, axis=1)

    @pl.when(waits_long())
    def _():
        product(own, recv, gate_own, m, wts, gate, y, wide)
        gated(y, gate, m, ROWS)


def late_kernel(m_in, own, recv, gate_own, gate_recv, m, wts, gate, y, wide):
    is_left = lax.rem(lax.axis_index("site"), 2) == 0

    @pl.when(jnp.logical_not(waits_long()))
    def _():
        @pl.when(is_left)
        def _():
            product(own, recv, gate_own, m, wts, gate, y, wide)

        @pl.when(jnp.logical_not(is_left))
        def _():
            product(recv, own, gate_recv, m, wts, gate, y, wide)

        gated(y, gate, m, ROWS)


def first_kernel(m, sk_own, sk_recv, out_a, out_b, s, st, wide, q, ab):
    is_left = lax.rem(lax.axis_index("site"), 2) == 0
    outs = (out_a, out_b)

    def sample(sketch):
        def some(i, _):
            rows = pl.ds(pl.multiple_of(i * HALF, HALF), HALF)
            s[rows, :] = dot(m[rows, :], sketch[:ROWS, :]).astype(BF16)
            return 0

        lax.fori_loop(0, 2, some, 0)

    @pl.when(is_left)
    def _():
        sample(sk_own)

    @pl.when(jnp.logical_not(is_left))
    def _():
        sample(sk_recv)

    st[...] = dot(identity(BF16), s[...], ((1,), (1,))).astype(BF16)
    ab[:, :CHI] = dot(st[...], s[...])

    def alongside(j):
        for t in (2 * j, 2 * j + 1):
            q[:, t * CHI : (t + 1) * CHI] = dot(st[...], m[:, t * CHI : (t + 1) * CHI]).astype(BF16)

    unscale = factor(ab, alongside)

    @pl.when(is_left)
    def _():
        made = dot(s[...], (ab[:, CHI:] * (unscale * LEFT_SCALE)).astype(BF16), ((1,), (1,)))
        for h in range(2):
            wide[h] = made[:, h * 128 : (h + 1) * 128]

        def put_out(h, u, value):
            outs[h][u * CHI : (u + 1) * CHI, :] = value

        take_slabs(wide, put_out)

    @pl.when(jnp.logical_not(is_left))
    def _():
        inv = (ab[:, CHI:] * (unscale * RIGHT_SCALE)).astype(BF16)
        for t in range(LEVELS):
            put_level(wide, t, dot(inv, q[:, t * CHI : (t + 1) * CHI]))
        for x in range(2):
            for h in range(2):
                outs[x][:, h * 128 : (h + 1) * 128] = wide[h, x * HALF : (x + 1) * HALF, :].astype(BF16)


def ready_kernel(sk_own, sk_recv, sk, gate):
    is_left, _ = role()

    def take(packed):
        sk[...] = packed[:ROWS, :]
        gate[...] = gate_matrix(packed[ROWS:, :])

    @pl.when(is_left)
    def _():
        take(sk_own)

    @pl.when(jnp.logical_not(is_left))
    def _():
        take(sk_recv)


def half_pair(own_a, own_b, recv, gate, y, m, is_left):
    owns = (own_a, own_b)

    @pl.when(is_left)
    def _():
        two_site(lambda p: owns[p][...], lambda p: recv, y, 0)

    @pl.when(jnp.logical_not(is_left))
    def _():
        block = recv[...]
        two_site(lambda p: block, lambda p: owns[p], y, 0)

    gated(y, gate, m, HALF)


def column_half(sk, sh, h):
    for t in range(LEVELS):
        at = t * CHI + h * 128
        sh[t * 128 : (t + 1) * 128, :] = sk[at : at + 128, :]


def sampled_rows(m, sh, g):
    lanes = [m[:, t * CHI + g * 128 : t * CHI + (g + 1) * 128] for t in range(LEVELS)]
    return dot(jnp.concatenate(lanes, axis=1), sh[...])


def role():
    me = lax.axis_index("site")
    return lax.rem(me, 2) == 1, (me > 0) & (me < lax.axis_size("site") - 1)


def mid_kernel(own_a, own_b, recv, sk, gate, acc, s0, m, sh, y):
    is_left, busy = role()

    @pl.when(busy)
    def _():
        half_pair(own_a, own_b, recv, gate, y, m, is_left)

        @pl.when(is_left)
        def _():
            column_half(sk, sh, 0)
            for g in range(2):
                acc[g * HALF : (g + 1) * HALF, :] = sampled_rows(m, sh, g)
            s0[...] = jnp.zeros_like(s0)

        @pl.when(jnp.logical_not(is_left))
        def _():
            s0[...] = dot(m[...], sk[...]).astype(BF16)


def last_kernel(
    own_a, own_b, recv, sk, gate, acc, s0, m0, out, sh, y, m, s, st, wide, q, ab
):
    is_left, busy = role()
    owns = (own_a, own_b)

    @pl.when(busy)
    def _():
        half_pair(own_a, own_b, recv, gate, y, m, is_left)

        @pl.when(is_left)
        def _():
            column_half(sk, sh, 1)
            for g in range(2):
                rows = slice(g * HALF, (g + 1) * HALF)
                s[rows, :] = (acc[rows, :] + sampled_rows(m, sh, g)).astype(BF16)

        @pl.when(jnp.logical_not(is_left))
        def _():
            s[:HALF, :] = s0[...]
            s[HALF:, :] = dot(m[...], sk[...]).astype(BF16)

        st[...] = dot(identity(BF16), s[...], ((1,), (1,))).astype(BF16)
        ab[:, :CHI] = dot(st[...], s[...])

        def alongside(j):
            for t in (2 * j, 2 * j + 1):
                columns = slice(t * CHI, (t + 1) * CHI)
                made = dot(st[:, :HALF], m0[:, columns]) + dot(st[:, HALF:], m[:, columns])
                q[:, columns] = made.astype(BF16)

        unscale = factor(ab, alongside)

        @pl.when(is_left)
        def _():
            out[...] = dot(s[...], (ab[:, CHI:] * (unscale * LEFT_SCALE)).astype(BF16), ((1,), (1,))).astype(BF16)

        @pl.when(jnp.logical_not(is_left))
        def _():
            inv = (ab[:, CHI:] * (unscale * RIGHT_SCALE)).astype(BF16)
            for t in range(LEVELS):
                put_level(wide, t, dot(inv, q[:, t * CHI : (t + 1) * CHI]))
            for h in range(2):
                out[:, h * 128 : (h + 1) * 128] = wide[h].astype(BF16)

    @pl.when(jnp.logical_not(busy))
    def _():
        @pl.when(is_left)
        def _():
            for x in range(2):
                out[x * HALF : (x + 1) * HALF, :] = owns[x][...]

        @pl.when(jnp.logical_not(is_left))
        def _():
            for h in range(2):
                for u in range(LEVELS // 2):
                    for e in range(2):
                        slab = owns[h][u * CHI : (u + 1) * CHI, e * 128 : (e + 1) * 128].astype(F32)
                        wide[h, pl.ds(2 * u + e, CHI, stride=LEVELS), :] = slab
            for h in range(2):
                out[:, h * 128 : (h + 1) * 128] = wide[h].astype(BF16)


HALF_ARRAY = jax.ShapeDtypeStruct((HALF, CHI), BF16)
WHOLE = pltpu.VMEM((ROWS, CHI), BF16)
TURNED = pltpu.VMEM((CHI, ROWS), BF16)
WIDE = pltpu.VMEM((2, ROWS, 128), F32)
GRAM = pltpu.VMEM((CHI, 2 * CHI), F32)
FACTOR = [WHOLE, TURNED, WIDE, TURNED, GRAM]
HALF_SCRATCH = [pltpu.VMEM((HALF, CHI), BF16), pltpu.VMEM((BONDS, GATE, CHI), BF16)]


def call(kernel, name, out_shape, scratch, limit, *args, aliases={}):
    single = not isinstance(out_shape, tuple)
    return pl.pallas_call(
        kernel,
        out_shape=out_shape,
        in_specs=[VMEM] * len(args),
        out_specs=VMEM if single else tuple(VMEM for _ in out_shape),
        scratch_shapes=scratch,
        input_output_aliases=aliases,
        compiler_params=pltpu.CompilerParams(vmem_limit_bytes=limit << 20),
        name=name,
    )(*args)


def per_device(site_tensors, first_gates, second_gates, first_sketch, second_sketch):
    devices = lax.axis_size("site")
    inside = [(i, i ^ 1) for i in range(devices)]
    across = [(i, (i + 1) % devices if i % 2 else (i - 1) % devices) for i in range(devices)]
    product_scratch = [
        pltpu.VMEM((2, HALF, CHI), BF16),
        pltpu.VMEM((4 * GATE, 4 * GATE), BF16),
        pltpu.VMEM((CHI, GATE, CHI), BF16),
        WIDE,
    ]
    whole_matrix = jax.ShapeDtypeStruct((ROWS, ROWS), BF16)
    half_matrix = jax.ShapeDtypeStruct((HALF, ROWS), BF16)
    whole_array = jax.ShapeDtypeStruct((ROWS, CHI), BF16)
    partial = jax.ShapeDtypeStruct((ROWS, CHI), F32)
    gate_shape = jax.ShapeDtypeStruct((4 * GATE, 4 * GATE), BF16)
    gate_rows_shape = jax.ShapeDtypeStruct((GATE, CHI), BF16)
    own = site_tensors[0].reshape(ROWS, CHI)
    recv = lax.ppermute(own, "site", inside)
    gate_recv = lax.ppermute(first_gates[0], "site", inside)
    sk0 = first_sketch[0].astype(BF16)
    sk0_recv = lax.ppermute(sk0, "site", inside)
    m, gate_rows = call(
        early_kernel,
        "early",
        (whole_matrix, gate_rows_shape),
        product_scratch,
        24,
        own,
        recv,
        first_gates[0],
        gate_recv,
        second_gates[0],
    )
    sk1 = jnp.concatenate([second_sketch[0].astype(BF16), gate_rows], axis=0)
    sk1_recv = lax.ppermute(sk1, "site", across)
    m = call(
        late_kernel,
        "late",
        whole_matrix,
        product_scratch,
        24,
        m,
        own,
        recv,
        first_gates[0],
        gate_recv,
        aliases={0: 0},
    )
    own_a, own_b = call(first_kernel, "first", (HALF_ARRAY, HALF_ARRAY), FACTOR, 24, m, sk0, sk0_recv)
    recv_a = lax.ppermute(own_a, "site", across)
    recv_b = lax.ppermute(own_b, "site", across)
    sk, gate = call(ready_kernel, "ready", (whole_array, gate_shape), [], 8, sk1, sk1_recv)
    acc, s0, m0 = call(
        mid_kernel, "mid", (partial, HALF_ARRAY, half_matrix), HALF_SCRATCH, 24, own_a, own_b, recv_a, sk, gate
    )
    last_scratch = [*HALF_SCRATCH, pltpu.VMEM((HALF, ROWS), BF16), *FACTOR]
    made = call(
        last_kernel, "last", whole_array, last_scratch, 32, own_a, own_b, recv_b, sk, gate, acc, s0, m0
    )
    return made.reshape(1, CHI, LEVELS, CHI)


def solution(mesh):
    in_specs = (
        P("site", None, None, None),
        P("site", None, None),
        P("site", None, None),
        P("site", None, None),
        P("site", None, None),
    )
    out_specs = P("site", None, None, None)
    return jax.shard_map(
        per_device, mesh=mesh, in_specs=in_specs, out_specs=out_specs, check_vma=False
    )
```

```python
import jax
import jax.numpy as jnp
from jax import lax
from jax.experimental import pallas as pl
from jax.experimental.pallas import tpu as pltpu
from jax.sharding import PartitionSpec as P

F32 = jnp.float32
BF16 = jnp.bfloat16
VMEM = pl.BlockSpec(memory_space=pltpu.VMEM)
CHI = 256
LEVELS = 8
ROWS = CHI * LEVELS
GATE = LEVELS * LEVELS
BLOCK = 64


def lanes_of(v, k):
    return jnp.broadcast_to(v[:, k : k + 1], (8, 128))


def row_of(v, r):
    return jnp.broadcast_to(v[r : r + 1, :], (8, 128))


def inverse_factor(diag_block):
    nb = BLOCK
    nv = nb // 8
    rows = lax.broadcasted_iota(jnp.int32, (nb, nb), 0)
    cols = lax.broadcasted_iota(jnp.int32, (nb, nb), 1)
    beside = jnp.concatenate([diag_block, jnp.where(rows == cols, 1.0, 0.0).astype(F32)], axis=1)
    v = [beside[8 * q : 8 * q + 8, :] for q in range(nv)]
    sub = lax.broadcasted_iota(jnp.int32, (8, 128), 0)
    scale = [jnp.ones((8, 128), F32)] * nv
    c = [[lanes_of(v[q], i) for q in range(nv)] for i in range(4)]
    for k in range(0, nb, 4):
        p, r = divmod(k, 8)
        last = k + 4 >= nb
        if not last:
            p2, r2 = divmod(k + 4, 8)
            ahead = [[lanes_of(v[q], k + 4 + i) for q in range(p2, nv)] for i in range(4)]
        row = [row_of(v[p], r + i) for i in range(4)]
        g = [[row_of(c[j][0], r + i) if i >= j else None for j in range(4)] for i in range(4)]
        a, b, d = g[0][0], g[1][0], g[1][1]
        det = a * d - b * b
        idet = 1.0 / det

        def adjugate(x, y):
            return x * d - y * b, y * a - x * b

        n20, n21 = adjugate(g[2][0], g[2][1])
        n30, n31 = adjugate(g[3][0], g[3][1])
        a2 = g[2][2] - (g[2][0] * n20 + g[2][1] * n21) * idet
        b2 = g[3][2] - (g[3][0] * n20 + g[3][1] * n21) * idet
        d2 = g[3][3] - (g[3][0] * n30 + g[3][1] * n31) * idet
        det2 = a2 * d2 - b2 * b2
        idet2 = 1.0 / det2
        m20, m21, m30, m31 = n20 * idet, n21 * idet, n30 * idet, n31 * idet

        def panel_solve(x0, x1, x2, x3):
            u0, u1 = adjugate(x0, x1)
            y2 = x2 - (m20 * x0 + m21 * x1)
            y3 = x3 - (m30 * x0 + m31 * x1)
            return u0 * idet, u1 * idet, (y2 * d2 - y3 * b2) * idet2, (y3 * a2 - y2 * b2) * idet2, y2, y3

        ce = [
            (
                c[0][q - p],
                c[1][q - p],
                c[2][q - p] - (m20 * c[0][q - p] + m21 * c[1][q - p]),
                c[3][q - p] - (m30 * c[0][q - p] + m31 * c[1][q - p]),
            )
            for q in range(p, nv)
        ]
        if not last:
            across = panel_solve(*[c[j][p2 - p] for j in range(4)])[:4]
            c_next = []
            for i in range(4):
                hs = [row_of(x, r2 + i) for x in across]
                c_next.append(
                    [
                        (ahead[i][q - p2] - (ce[q - p][0] * hs[0] + ce[q - p][1] * hs[1]))
                        - (ce[q - p][2] * hs[2] + ce[q - p][3] * hs[3])
                        for q in range(p2, nv)
                    ]
                )
        u0, u1, h2, h3, row2, row3 = panel_solve(*row)
        below = sub > r + 3
        for q in range(p, nv):
            cq = ce[q - p]
            if q == p:
                cq = [jnp.where(below, x, 0.0) for x in cq]
            v[q] = (v[q] - (cq[0] * u0 + cq[1] * u1)) - (cq[2] * h2 + cq[3] * h3)
        ia = 1.0 / a
        ia2 = 1.0 / a2
        row1 = row[1] - (b * ia) * row[0]
        row3 = row3 - (b2 * ia2) * row2
        v[p] = jnp.where(
            sub == r + 1, row1, jnp.where(sub == r + 2, row2, jnp.where(sub == r + 3, row3, v[p]))
        )
        scale[p] = jnp.where(
            sub == r,
            lax.rsqrt(a),
            jnp.where(
                sub == r + 1,
                lax.rsqrt(det * ia),
                jnp.where(sub == r + 2, lax.rsqrt(a2), jnp.where(sub == r + 3, lax.rsqrt(det2 * ia2), scale[p])),
            ),
        )
        if not last:
            c = c_next
    return jnp.concatenate([v[q] * scale[q] for q in range(nv)], axis=0)


def dot(x, y, dims=((1,), (0,))):
    return lax.dot_general(x, y, (dims, ((), ())), preferred_element_type=F32)


def dot_split(x, y, dims=((1,), (0,))):
    xh = x.astype(BF16)
    xl = (x - xh.astype(F32)).astype(BF16)
    yh = y.astype(BF16)
    yl = (y - yh.astype(F32)).astype(BF16)
    return dot(xh, yh, dims) + (dot(xh, yl, dims) + dot(xl, yh, dims))


def gate_matrix(packed):
    i = lax.broadcasted_iota(jnp.int32, (GATE, GATE), 0)
    j = lax.broadcasted_iota(jnp.int32, (GATE, GATE), 1)
    swap = jnp.where(j == (i & 7) * 8 + (i >> 3), 1.0, 0.0).astype(BF16)
    g = dot(dot(swap, packed[:, :GATE]).astype(BF16), swap, ((1,), (1,))).astype(BF16)
    wide = jnp.concatenate([jnp.concatenate([g] * 4, axis=1)] * 4, axis=0)
    big_i = lax.broadcasted_iota(jnp.int32, (4 * GATE, 4 * GATE), 0)
    big_j = lax.broadcasted_iota(jnp.int32, (4 * GATE, 4 * GATE), 1)
    return jnp.where((big_i >> 6) == (big_j >> 6), wide, jnp.zeros_like(wide))


HALF = ROWS // 2
ROW_SITES = 8
BONDS = CHI // 2
STEP = 512


def put_level(wide, t, value):
    for h in range(2):
        wide[h, pl.ds(t, CHI, stride=LEVELS), :] = value[:, h * 128 : (h + 1) * 128]


def take_slabs(wide, put):
    for h in range(2):
        for u in range(LEVELS // 2):
            pair = [wide[h, pl.ds(2 * u + e, CHI, stride=LEVELS), :] for e in range(2)]
            put(h, u, jnp.concatenate(pair, axis=1).astype(BF16))


def identity(dtype):
    i = lax.broadcasted_iota(jnp.int32, (CHI, CHI), 0)
    j = lax.broadcasted_iota(jnp.int32, (CHI, CHI), 1)
    return jnp.where(i == j, 1.0, 0.0).astype(dtype)


def two_site(lhs_of, weights_of, y, a0):
    for p in range(2):
        block, weights = lhs_of(p), weights_of(p)
        for u in range(LEVELS // 2):
            made = dot(block, weights[u * CHI : (u + 1) * CHI, :]).reshape(BONDS, LEVELS, CHI)
            both = jnp.concatenate([made[:, :, :128], made[:, :, 128:]], axis=1).astype(BF16)
            y[pl.ds(a0, BONDS), 16 * u : 16 * u + 16, p * 128 : (p + 1) * 128] = both


def gated(y, gate, m, rows):
    bonds = STEP // LEVELS

    def some(i, _):
        r0 = pl.multiple_of(i * STEP, STEP)
        a0 = pl.multiple_of(i * bonds, bonds)
        for j in range(bonds // 4):
            four = y[pl.ds(a0 + 4 * j, 4)].reshape(4 * GATE, CHI)
            o = dot(gate[...], four).reshape(4, LEVELS, LEVELS, CHI)
            for h in range(2):
                at = pl.multiple_of(r0 + j * 32 + h * 16, 16)
                for t in range(LEVELS):
                    m[pl.ds(at, 16), t * CHI : (t + 1) * CHI] = jnp.concatenate(
                        [o[2 * h, t], o[2 * h + 1, t]], axis=0
                    ).astype(BF16)
        return 0

    lax.fori_loop(0, rows // STEP, some, 0)


def factor(ab, alongside):
    unit = identity(F32)
    gram = ab[:, :CHI]
    largest = jnp.max(gram * unit, keepdims=True)
    ab[:, :CHI] = gram * (1.0 / largest)
    ab[:, CHI:] = unit
    lane = lax.broadcasted_iota(jnp.int32, (BLOCK, 128), 1)
    none = jnp.zeros((BLOCK, 2 * CHI), F32)
    block = ab[:BLOCK, :BLOCK]
    for o in range(0, CHI, BLOCK):
        e = o + BLOCK
        uw = inverse_factor(block)
        alongside(o // BLOCK)
        panel = dot_split(uw, jnp.concatenate([none, ab[o:e, :]], axis=0))
        ab[o:e, CHI:] = panel[:, CHI:]
        if e < CHI:
            tile = o // 128 * 128
            if o == tile:
                w = jnp.concatenate([uw[:, BLOCK:], jnp.zeros((BLOCK, BLOCK), F32)], axis=1)
            else:
                w = jnp.where(lane >= BLOCK, uw, 0.0)
            turned = dot_split(ab[e:, tile : tile + 128], w, ((1,), (1,)))
            top = ab[e : e + BLOCK, :] - dot_split(turned[:BLOCK], panel)
            block = top[:, e : e + BLOCK]
            ab[e : e + BLOCK, :] = top
            if e + BLOCK < CHI:
                ab[e + BLOCK :, :] = ab[e + BLOCK :, :] - dot_split(turned[BLOCK:], panel)
    return lax.rsqrt(largest)


LEFT_SCALE = LEVELS**0.5 * CHI**0.25
RIGHT_SCALE = LEFT_SCALE * ROWS**-0.5


def waits_long():
    return lax.rem(lax.axis_index("site"), ROW_SITES) == 0


def product(left, right, y, wts, wide):
    for h in range(2):
        wide[h] = right[:, h * 128 : (h + 1) * 128].astype(F32)

    def put(h, u, value):
        wts[h, u * CHI : (u + 1) * CHI, :] = value

    take_slabs(wide, put)

    def some(x, _):
        block = left[pl.ds(pl.multiple_of(x * HALF, HALF), HALF), :]
        two_site(lambda p: block, lambda p: wts.at[p], y, pl.multiple_of(x * BONDS, BONDS))
        return 0

    lax.fori_loop(0, 2, some, 0)


def early_kernel(own, recv, gate_own, gate_recv, gate_next, y, gate, gate_rows, wts, wide):
    gate_rows[...] = jnp.concatenate([gate_next[...]] * 4, axis=1)

    @pl.when(waits_long())
    def _():
        gate[...] = gate_matrix(gate_own[...])
        product(own, recv, y, wts, wide)


def late_kernel(y_in, gate_in, own, recv, gate_own, gate_recv, y, gate, m, wts, wide):
    is_left = lax.rem(lax.axis_index("site"), 2) == 0

    @pl.when(jnp.logical_not(waits_long()))
    def _():
        @pl.when(is_left)
        def _():
            gate[...] = gate_matrix(gate_own[...])
            product(own, recv, y, wts, wide)

        @pl.when(jnp.logical_not(is_left))
        def _():
            gate[...] = gate_matrix(gate_recv[...])
            product(recv, own, y, wts, wide)

    gated(y, gate, m, ROWS)


def first_kernel(m, sk_own, sk_recv, out_a, out_b, s, st, wide, q, ab):
    is_left = lax.rem(lax.axis_index("site"), 2) == 0
    outs = (out_a, out_b)

    def sample(sketch):
        def some(i, _):
            rows = pl.ds(pl.multiple_of(i * HALF, HALF), HALF)
            s[rows, :] = dot(m[rows, :], sketch[:ROWS, :]).astype(BF16)
            return 0

        lax.fori_loop(0, 2, some, 0)

    @pl.when(is_left)
    def _():
        sample(sk_own)

    @pl.when(jnp.logical_not(is_left))
    def _():
        sample(sk_recv)

    st[...] = dot(identity(BF16), s[...], ((1,), (1,))).astype(BF16)
    ab[:, :CHI] = dot(st[...], s[...])

    def alongside(j):
        for t in (2 * j, 2 * j + 1):
            q[:, t * CHI : (t + 1) * CHI] = dot(st[...], m[:, t * CHI : (t + 1) * CHI]).astype(BF16)

    unscale = factor(ab, alongside)

    @pl.when(is_left)
    def _():
        made = dot(s[...], (ab[:, CHI:] * (unscale * LEFT_SCALE)).astype(BF16), ((1,), (1,)))
        for h in range(2):
            wide[h] = made[:, h * 128 : (h + 1) * 128]

        def put_out(h, u, value):
            outs[h][u * CHI : (u + 1) * CHI, :] = value

        take_slabs(wide, put_out)

    @pl.when(jnp.logical_not(is_left))
    def _():
        inv = (ab[:, CHI:] * (unscale * RIGHT_SCALE)).astype(BF16)
        for t in range(LEVELS):
            put_level(wide, t, dot(inv, q[:, t * CHI : (t + 1) * CHI]))
        for x in range(2):
            for h in range(2):
                outs[x][:, h * 128 : (h + 1) * 128] = wide[h, x * HALF : (x + 1) * HALF, :].astype(BF16)


def ready_kernel(sk_own, sk_recv, sk, gate):
    is_left, _ = role()

    def take(packed):
        sk[...] = packed[:ROWS, :]
        gate[...] = gate_matrix(packed[ROWS:, :])

    @pl.when(is_left)
    def _():
        take(sk_own)

    @pl.when(jnp.logical_not(is_left))
    def _():
        take(sk_recv)


def half_pair(own_a, own_b, recv, gate, y, m, is_left):
    owns = (own_a, own_b)

    @pl.when(is_left)
    def _():
        two_site(lambda p: owns[p][...], lambda p: recv, y, 0)

    @pl.when(jnp.logical_not(is_left))
    def _():
        block = recv[...]
        two_site(lambda p: block, lambda p: owns[p], y, 0)

    gated(y, gate, m, HALF)


def column_half(sk, sh, h):
    for t in range(LEVELS):
        at = t * CHI + h * 128
        sh[t * 128 : (t + 1) * 128, :] = sk[at : at + 128, :]


def sampled_rows(m, sh, g):
    lanes = [m[:, t * CHI + g * 128 : t * CHI + (g + 1) * 128] for t in range(LEVELS)]
    return dot(jnp.concatenate(lanes, axis=1), sh[...])


def role():
    me = lax.axis_index("site")
    return lax.rem(me, 2) == 1, (me > 0) & (me < lax.axis_size("site") - 1)


def mid_kernel(own_a, own_b, recv, sk, gate, acc, s0, m, sh, y):
    is_left, busy = role()

    @pl.when(busy)
    def _():
        half_pair(own_a, own_b, recv, gate, y, m, is_left)

        @pl.when(is_left)
        def _():
            column_half(sk, sh, 0)
            for g in range(2):
                acc[g * HALF : (g + 1) * HALF, :] = sampled_rows(m, sh, g)
            s0[...] = jnp.zeros_like(s0)

        @pl.when(jnp.logical_not(is_left))
        def _():
            s0[...] = dot(m[...], sk[...]).astype(BF16)


def last_kernel(
    own_a, own_b, recv, sk, gate, acc, s0, m0, out, sh, y, m, s, st, wide, q, ab
):
    is_left, busy = role()
    owns = (own_a, own_b)

    @pl.when(busy)
    def _():
        half_pair(own_a, own_b, recv, gate, y, m, is_left)

        @pl.when(is_left)
        def _():
            column_half(sk, sh, 1)
            for g in range(2):
                rows = slice(g * HALF, (g + 1) * HALF)
                s[rows, :] = (acc[rows, :] + sampled_rows(m, sh, g)).astype(BF16)

        @pl.when(jnp.logical_not(is_left))
        def _():
            s[:HALF, :] = s0[...]
            s[HALF:, :] = dot(m[...], sk[...]).astype(BF16)

        st[...] = dot(identity(BF16), s[...], ((1,), (1,))).astype(BF16)
        ab[:, :CHI] = dot(st[...], s[...])

        def alongside(j):
            for t in (2 * j, 2 * j + 1):
                columns = slice(t * CHI, (t + 1) * CHI)
                made = dot(st[:, :HALF], m0[:, columns]) + dot(st[:, HALF:], m[:, columns])
                q[:, columns] = made.astype(BF16)

        unscale = factor(ab, alongside)

        @pl.when(is_left)
        def _():
            out[...] = dot(s[...], (ab[:, CHI:] * (unscale * LEFT_SCALE)).astype(BF16), ((1,), (1,))).astype(BF16)

        @pl.when(jnp.logical_not(is_left))
        def _():
            inv = (ab[:, CHI:] * (unscale * RIGHT_SCALE)).astype(BF16)
            for t in range(LEVELS):
                put_level(wide, t, dot(inv, q[:, t * CHI : (t + 1) * CHI]))
            for h in range(2):
                out[:, h * 128 : (h + 1) * 128] = wide[h].astype(BF16)

    @pl.when(jnp.logical_not(busy))
    def _():
        @pl.when(is_left)
        def _():
            for x in range(2):
                out[x * HALF : (x + 1) * HALF, :] = owns[x][...]

        @pl.when(jnp.logical_not(is_left))
        def _():
            for h in range(2):
                for u in range(LEVELS // 2):
                    for e in range(2):
                        slab = owns[h][u * CHI : (u + 1) * CHI, e * 128 : (e + 1) * 128].astype(F32)
                        wide[h, pl.ds(2 * u + e, CHI, stride=LEVELS), :] = slab
            for h in range(2):
                out[:, h * 128 : (h + 1) * 128] = wide[h].astype(BF16)


HALF_ARRAY = jax.ShapeDtypeStruct((HALF, CHI), BF16)
WHOLE = pltpu.VMEM((ROWS, CHI), BF16)
TURNED = pltpu.VMEM((CHI, ROWS), BF16)
WIDE = pltpu.VMEM((2, ROWS, 128), F32)
GRAM = pltpu.VMEM((CHI, 2 * CHI), F32)
FACTOR = [WHOLE, TURNED, WIDE, TURNED, GRAM]
HALF_SCRATCH = [pltpu.VMEM((HALF, CHI), BF16), pltpu.VMEM((BONDS, GATE, CHI), BF16)]


def call(kernel, name, out_shape, scratch, limit, *args, aliases={}):
    single = not isinstance(out_shape, tuple)
    return pl.pallas_call(
        kernel,
        out_shape=out_shape,
        in_specs=[VMEM] * len(args),
        out_specs=VMEM if single else tuple(VMEM for _ in out_shape),
        scratch_shapes=scratch,
        input_output_aliases=aliases,
        compiler_params=pltpu.CompilerParams(vmem_limit_bytes=limit << 20),
        name=name,
    )(*args)


def per_device(site_tensors, first_gates, second_gates, first_sketch, second_sketch):
    devices = lax.axis_size("site")
    inside = [(i, i ^ 1) for i in range(devices)]
    across = [(i, (i + 1) % devices if i % 2 else (i - 1) % devices) for i in range(devices)]
    product_scratch = [pltpu.VMEM((2, HALF, CHI), BF16), WIDE]
    whole_matrix = jax.ShapeDtypeStruct((ROWS, ROWS), BF16)
    half_matrix = jax.ShapeDtypeStruct((HALF, ROWS), BF16)
    whole_array = jax.ShapeDtypeStruct((ROWS, CHI), BF16)
    partial = jax.ShapeDtypeStruct((ROWS, CHI), F32)
    gate_shape = jax.ShapeDtypeStruct((4 * GATE, 4 * GATE), BF16)
    gate_rows_shape = jax.ShapeDtypeStruct((GATE, CHI), BF16)
    product_shape = jax.ShapeDtypeStruct((CHI, GATE, CHI), BF16)
    own = site_tensors[0].reshape(ROWS, CHI)
    recv = lax.ppermute(own, "site", inside)
    gate_recv = lax.ppermute(first_gates[0], "site", inside)
    sk0 = first_sketch[0].astype(BF16)
    sk0_recv = lax.ppermute(sk0, "site", inside)
    y, gate, gate_rows = call(
        early_kernel,
        "early",
        (product_shape, gate_shape, gate_rows_shape),
        product_scratch,
        24,
        own,
        recv,
        first_gates[0],
        gate_recv,
        second_gates[0],
    )
    sk1 = jnp.concatenate([second_sketch[0].astype(BF16), gate_rows], axis=0)
    sk1_recv = lax.ppermute(sk1, "site", across)
    _, _, m = call(
        late_kernel,
        "late",
        (product_shape, gate_shape, whole_matrix),
        product_scratch,
        24,
        y,
        gate,
        own,
        recv,
        first_gates[0],
        gate_recv,
        aliases={0: 0, 1: 1},
    )
    own_a, own_b = call(first_kernel, "first", (HALF_ARRAY, HALF_ARRAY), FACTOR, 24, m, sk0, sk0_recv)
    recv_a = lax.ppermute(own_a, "site", across)
    recv_b = lax.ppermute(own_b, "site", across)
    sk, gate = call(ready_kernel, "ready", (whole_array, gate_shape), [], 8, sk1, sk1_recv)
    acc, s0, m0 = call(
        mid_kernel, "mid", (partial, HALF_ARRAY, half_matrix), HALF_SCRATCH, 24, own_a, own_b, recv_a, sk, gate
    )
    last_scratch = [*HALF_SCRATCH, pltpu.VMEM((HALF, ROWS), BF16), *FACTOR]
    made = call(
        last_kernel, "last", whole_array, last_scratch, 32, own_a, own_b, recv_b, sk, gate, acc, s0, m0
    )
    return made.reshape(1, CHI, LEVELS, CHI)


def solution(mesh):
    in_specs = (
        P("site", None, None, None),
        P("site", None, None),
        P("site", None, None),
        P("site", None, None),
        P("site", None, None),
    )
    out_specs = P("site", None, None, None)
    return jax.shard_map(
        per_device, mesh=mesh, in_specs=in_specs, out_specs=out_specs, check_vma=False
    )
```

```python
import jax
import jax.numpy as jnp
from jax import lax
from jax.experimental import pallas as pl
from jax.experimental.pallas import tpu as pltpu
from jax.sharding import PartitionSpec as P

F32 = jnp.float32
BF16 = jnp.bfloat16
VMEM = pl.BlockSpec(memory_space=pltpu.VMEM)
CHI = 256
LEVELS = 8
ROWS = CHI * LEVELS
GATE = LEVELS * LEVELS
BLOCK = 64


def lanes_of(v, k):
    return jnp.broadcast_to(v[:, k : k + 1], (8, 128))


def row_of(v, r):
    return jnp.broadcast_to(v[r : r + 1, :], (8, 128))


def inverse_factor(diag_block):
    nb = BLOCK
    nv = nb // 8
    rows = lax.broadcasted_iota(jnp.int32, (nb, nb), 0)
    cols = lax.broadcasted_iota(jnp.int32, (nb, nb), 1)
    beside = jnp.concatenate([diag_block, jnp.where(rows == cols, 1.0, 0.0).astype(F32)], axis=1)
    v = [beside[8 * q : 8 * q + 8, :] for q in range(nv)]
    sub = lax.broadcasted_iota(jnp.int32, (8, 128), 0)
    scale = [jnp.ones((8, 128), F32)] * nv
    c = [[lanes_of(v[q], i) for q in range(nv)] for i in range(4)]
    for k in range(0, nb, 4):
        p, r = divmod(k, 8)
        last = k + 4 >= nb
        if not last:
            p2, r2 = divmod(k + 4, 8)
            ahead = [[lanes_of(v[q], k + 4 + i) for q in range(p2, nv)] for i in range(4)]
        row = [row_of(v[p], r + i) for i in range(4)]
        g = [[row_of(c[j][0], r + i) if i >= j else None for j in range(4)] for i in range(4)]
        a, b, d = g[0][0], g[1][0], g[1][1]
        det = a * d - b * b
        idet = 1.0 / det

        def adjugate(x, y):
            return x * d - y * b, y * a - x * b

        n20, n21 = adjugate(g[2][0], g[2][1])
        n30, n31 = adjugate(g[3][0], g[3][1])
        a2 = g[2][2] - (g[2][0] * n20 + g[2][1] * n21) * idet
        b2 = g[3][2] - (g[3][0] * n20 + g[3][1] * n21) * idet
        d2 = g[3][3] - (g[3][0] * n30 + g[3][1] * n31) * idet
        det2 = a2 * d2 - b2 * b2
        idet2 = 1.0 / det2
        m20, m21, m30, m31 = n20 * idet, n21 * idet, n30 * idet, n31 * idet

        def panel_solve(x0, x1, x2, x3):
            u0, u1 = adjugate(x0, x1)
            y2 = x2 - (m20 * x0 + m21 * x1)
            y3 = x3 - (m30 * x0 + m31 * x1)
            return u0 * idet, u1 * idet, (y2 * d2 - y3 * b2) * idet2, (y3 * a2 - y2 * b2) * idet2, y2, y3

        ce = [
            (
                c[0][q - p],
                c[1][q - p],
                c[2][q - p] - (m20 * c[0][q - p] + m21 * c[1][q - p]),
                c[3][q - p] - (m30 * c[0][q - p] + m31 * c[1][q - p]),
            )
            for q in range(p, nv)
        ]
        if not last:
            across = panel_solve(*[c[j][p2 - p] for j in range(4)])[:4]
            c_next = []
            for i in range(4):
                hs = [row_of(x, r2 + i) for x in across]
                c_next.append(
                    [
                        (ahead[i][q - p2] - (ce[q - p][0] * hs[0] + ce[q - p][1] * hs[1]))
                        - (ce[q - p][2] * hs[2] + ce[q - p][3] * hs[3])
                        for q in range(p2, nv)
                    ]
                )
        u0, u1, h2, h3, row2, row3 = panel_solve(*row)
        below = sub > r + 3
        for q in range(p, nv):
            cq = ce[q - p]
            if q == p:
                cq = [jnp.where(below, x, 0.0) for x in cq]
            v[q] = (v[q] - (cq[0] * u0 + cq[1] * u1)) - (cq[2] * h2 + cq[3] * h3)
        ia = 1.0 / a
        ia2 = 1.0 / a2
        row1 = row[1] - (b * ia) * row[0]
        row3 = row3 - (b2 * ia2) * row2
        v[p] = jnp.where(
            sub == r + 1, row1, jnp.where(sub == r + 2, row2, jnp.where(sub == r + 3, row3, v[p]))
        )
        scale[p] = jnp.where(
            sub == r,
            lax.rsqrt(a),
            jnp.where(
                sub == r + 1,
                lax.rsqrt(det * ia),
                jnp.where(sub == r + 2, lax.rsqrt(a2), jnp.where(sub == r + 3, lax.rsqrt(det2 * ia2), scale[p])),
            ),
        )
        if not last:
            c = c_next
    return jnp.concatenate([v[q] * scale[q] for q in range(nv)], axis=0)


def dot(x, y, dims=((1,), (0,))):
    return lax.dot_general(x, y, (dims, ((), ())), preferred_element_type=F32)


def dot_split(x, y, dims=((1,), (0,))):
    xh = x.astype(BF16)
    xl = (x - xh.astype(F32)).astype(BF16)
    yh = y.astype(BF16)
    yl = (y - yh.astype(F32)).astype(BF16)
    return dot(xh, yh, dims) + (dot(xh, yl, dims) + dot(xl, yh, dims))


def gate_matrix(packed):
    i = lax.broadcasted_iota(jnp.int32, (GATE, GATE), 0)
    j = lax.broadcasted_iota(jnp.int32, (GATE, GATE), 1)
    swap = jnp.where(j == (i & 7) * 8 + (i >> 3), 1.0, 0.0).astype(BF16)
    g = dot(dot(swap, packed[:, :GATE]).astype(BF16), swap, ((1,), (1,))).astype(BF16)
    wide = jnp.concatenate([jnp.concatenate([g] * 4, axis=1)] * 4, axis=0)
    big_i = lax.broadcasted_iota(jnp.int32, (4 * GATE, 4 * GATE), 0)
    big_j = lax.broadcasted_iota(jnp.int32, (4 * GATE, 4 * GATE), 1)
    return jnp.where((big_i >> 6) == (big_j >> 6), wide, jnp.zeros_like(wide))


HALF = ROWS // 2
ROW_SITES = 32
BONDS = CHI // 2
STEP = 512


def put_level(wide, t, value):
    for h in range(2):
        wide[h, pl.ds(t, CHI, stride=LEVELS), :] = value[:, h * 128 : (h + 1) * 128]


def take_slabs(wide, put):
    for h in range(2):
        for u in range(LEVELS // 2):
            pair = [wide[h, pl.ds(2 * u + e, CHI, stride=LEVELS), :] for e in range(2)]
            put(h, u, jnp.concatenate(pair, axis=1).astype(BF16))


def identity(dtype):
    i = lax.broadcasted_iota(jnp.int32, (CHI, CHI), 0)
    j = lax.broadcasted_iota(jnp.int32, (CHI, CHI), 1)
    return jnp.where(i == j, 1.0, 0.0).astype(dtype)


def two_site(lhs_of, weights_of, y, a0):
    for p in range(2):
        block, weights = lhs_of(p), weights_of(p)
        for u in range(LEVELS // 2):
            made = dot(block, weights[u * CHI : (u + 1) * CHI, :]).reshape(BONDS, LEVELS, CHI)
            both = jnp.concatenate([made[:, :, :128], made[:, :, 128:]], axis=1).astype(BF16)
            y[pl.ds(a0, BONDS), 16 * u : 16 * u + 16, p * 128 : (p + 1) * 128] = both


def gated(y, gate, m, rows):
    bonds = STEP // LEVELS

    def some(i, _):
        r0 = pl.multiple_of(i * STEP, STEP)
        a0 = pl.multiple_of(i * bonds, bonds)
        for j in range(bonds // 4):
            four = y[pl.ds(a0 + 4 * j, 4)].reshape(4 * GATE, CHI)
            o = dot(gate[...], four).reshape(4, LEVELS, LEVELS, CHI)
            for h in range(2):
                at = pl.multiple_of(r0 + j * 32 + h * 16, 16)
                for t in range(LEVELS):
                    m[pl.ds(at, 16), t * CHI : (t + 1) * CHI] = jnp.concatenate(
                        [o[2 * h, t], o[2 * h + 1, t]], axis=0
                    ).astype(BF16)
        return 0

    lax.fori_loop(0, rows // STEP, some, 0)


def factor(ab, alongside):
    unit = identity(F32)
    gram = ab[:, :CHI]
    largest = jnp.max(gram * unit, keepdims=True)
    ab[:, :CHI] = gram * (1.0 / largest)
    ab[:, CHI:] = unit
    lane = lax.broadcasted_iota(jnp.int32, (BLOCK, 128), 1)
    none = jnp.zeros((BLOCK, 2 * CHI), F32)
    block = ab[:BLOCK, :BLOCK]
    for o in range(0, CHI, BLOCK):
        e = o + BLOCK
        uw = inverse_factor(block)
        alongside(o // BLOCK)
        panel = dot_split(uw, jnp.concatenate([none, ab[o:e, :]], axis=0))
        ab[o:e, CHI:] = panel[:, CHI:]
        if e < CHI:
            tile = o // 128 * 128
            if o == tile:
                w = jnp.concatenate([uw[:, BLOCK:], jnp.zeros((BLOCK, BLOCK), F32)], axis=1)
            else:
                w = jnp.where(lane >= BLOCK, uw, 0.0)
            turned = dot_split(ab[e:, tile : tile + 128], w, ((1,), (1,)))
            top = ab[e : e + BLOCK, :] - dot_split(turned[:BLOCK], panel)
            block = top[:, e : e + BLOCK]
            ab[e : e + BLOCK, :] = top
            if e + BLOCK < CHI:
                ab[e + BLOCK :, :] = ab[e + BLOCK :, :] - dot_split(turned[BLOCK:], panel)
    return lax.rsqrt(largest)


LEFT_SCALE = LEVELS**0.5 * CHI**0.25
RIGHT_SCALE = LEFT_SCALE * ROWS**-0.5


def waits_long():
    return lax.rem(lax.axis_index("site"), ROW_SITES) == 0


def product(left, right, y, wts, wide):
    for h in range(2):
        wide[h] = right[:, h * 128 : (h + 1) * 128].astype(F32)

    def put(h, u, value):
        wts[h, u * CHI : (u + 1) * CHI, :] = value

    take_slabs(wide, put)

    def some(x, _):
        block = left[pl.ds(pl.multiple_of(x * HALF, HALF), HALF), :]
        two_site(lambda p: block, lambda p: wts.at[p], y, pl.multiple_of(x * BONDS, BONDS))
        return 0

    lax.fori_loop(0, 2, some, 0)


def early_kernel(own, recv, gate_own, gate_recv, gate_next, y, gate, gate_rows, wts, wide):
    gate_rows[...] = jnp.concatenate([gate_next[...]] * 4, axis=1)

    @pl.when(waits_long())
    def _():
        gate[...] = gate_matrix(gate_own[...])
        product(own, recv, y, wts, wide)


def late_kernel(y_in, gate_in, own, recv, gate_own, gate_recv, y, gate, m, wts, wide):
    is_left = lax.rem(lax.axis_index("site"), 2) == 0

    @pl.when(jnp.logical_not(waits_long()))
    def _():
        @pl.when(is_left)
        def _():
            gate[...] = gate_matrix(gate_own[...])
            product(own, recv, y, wts, wide)

        @pl.when(jnp.logical_not(is_left))
        def _():
            gate[...] = gate_matrix(gate_recv[...])
            product(recv, own, y, wts, wide)

    gated(y, gate, m, ROWS)


def first_kernel(m, sk_own, sk_recv, out_a, out_b, sk, s, st, wide, q, ab):
    is_left = lax.rem(lax.axis_index("site"), 2) == 0
    outs = (out_a, out_b)

    @pl.when(is_left)
    def _():
        sk[...] = sk_own[...].astype(F32).astype(BF16)

    @pl.when(jnp.logical_not(is_left))
    def _():
        sk[...] = sk_recv[...].astype(F32).astype(BF16)

    def sample(i, _):
        rows = pl.ds(pl.multiple_of(i * HALF, HALF), HALF)
        s[rows, :] = dot(m[rows, :], sk[...]).astype(BF16)
        return 0

    lax.fori_loop(0, 2, sample, 0)
    st[...] = dot(identity(BF16), s[...], ((1,), (1,))).astype(BF16)
    ab[:, :CHI] = dot(st[...], s[...])

    def alongside(j):
        for t in (2 * j, 2 * j + 1):
            q[:, t * CHI : (t + 1) * CHI] = dot(st[...], m[:, t * CHI : (t + 1) * CHI]).astype(BF16)

    unscale = factor(ab, alongside)

    @pl.when(is_left)
    def _():
        made = dot(s[...], (ab[:, CHI:] * (unscale * LEFT_SCALE)).astype(BF16), ((1,), (1,)))
        for h in range(2):
            wide[h] = made[:, h * 128 : (h + 1) * 128]

        def put_out(h, u, value):
            outs[h][u * CHI : (u + 1) * CHI, :] = value

        take_slabs(wide, put_out)

    @pl.when(jnp.logical_not(is_left))
    def _():
        inv = (ab[:, CHI:] * (unscale * RIGHT_SCALE)).astype(BF16)
        for t in range(LEVELS):
            put_level(wide, t, dot(inv, q[:, t * CHI : (t + 1) * CHI]))
        for x in range(2):
            for h in range(2):
                outs[x][:, h * 128 : (h + 1) * 128] = wide[h, x * HALF : (x + 1) * HALF, :].astype(BF16)


def ready_kernel(sk_own, sk_recv, sk, gate):
    is_left, _ = role()

    def take(packed):
        sk[...] = packed[:ROWS, :]
        gate[...] = gate_matrix(packed[ROWS:, :])

    @pl.when(is_left)
    def _():
        take(sk_own)

    @pl.when(jnp.logical_not(is_left))
    def _():
        take(sk_recv)


def half_pair(own_a, own_b, recv, gate, y, m, is_left):
    owns = (own_a, own_b)

    @pl.when(is_left)
    def _():
        two_site(lambda p: owns[p][...], lambda p: recv, y, 0)

    @pl.when(jnp.logical_not(is_left))
    def _():
        block = recv[...]
        two_site(lambda p: block, lambda p: owns[p], y, 0)

    gated(y, gate, m, HALF)


def column_half(sk, sh, h):
    for t in range(LEVELS):
        at = t * CHI + h * 128
        sh[t * 128 : (t + 1) * 128, :] = sk[at : at + 128, :]


def sampled_rows(m, sh, g):
    lanes = [m[:, t * CHI + g * 128 : t * CHI + (g + 1) * 128] for t in range(LEVELS)]
    return dot(jnp.concatenate(lanes, axis=1), sh[...])


def role():
    me = lax.axis_index("site")
    return lax.rem(me, 2) == 1, (me > 0) & (me < lax.axis_size("site") - 1)


def mid_kernel(own_a, own_b, recv, sk, gate, acc, s0, m, sh, y):
    is_left, busy = role()

    @pl.when(busy)
    def _():
        half_pair(own_a, own_b, recv, gate, y, m, is_left)

        @pl.when(is_left)
        def _():
            column_half(sk, sh, 0)
            for g in range(2):
                acc[g * HALF : (g + 1) * HALF, :] = sampled_rows(m, sh, g)
            s0[...] = jnp.zeros_like(s0)

        @pl.when(jnp.logical_not(is_left))
        def _():
            s0[...] = dot(m[...], sk[...]).astype(BF16)


def last_kernel(
    own_a, own_b, recv, sk, gate, acc, s0, m0, out, sh, y, m, s, st, wide, q, ab
):
    is_left, busy = role()
    owns = (own_a, own_b)

    @pl.when(busy)
    def _():
        half_pair(own_a, own_b, recv, gate, y, m, is_left)

        @pl.when(is_left)
        def _():
            column_half(sk, sh, 1)
            for g in range(2):
                rows = slice(g * HALF, (g + 1) * HALF)
                s[rows, :] = (acc[rows, :] + sampled_rows(m, sh, g)).astype(BF16)

        @pl.when(jnp.logical_not(is_left))
        def _():
            s[:HALF, :] = s0[...]
            s[HALF:, :] = dot(m[...], sk[...]).astype(BF16)

        st[...] = dot(identity(BF16), s[...], ((1,), (1,))).astype(BF16)
        ab[:, :CHI] = dot(st[...], s[...])

        def alongside(j):
            for t in (2 * j, 2 * j + 1):
                columns = slice(t * CHI, (t + 1) * CHI)
                made = dot(st[:, :HALF], m0[:, columns]) + dot(st[:, HALF:], m[:, columns])
                q[:, columns] = made.astype(BF16)

        unscale = factor(ab, alongside)

        @pl.when(is_left)
        def _():
            out[...] = dot(s[...], (ab[:, CHI:] * (unscale * LEFT_SCALE)).astype(BF16), ((1,), (1,))).astype(BF16)

        @pl.when(jnp.logical_not(is_left))
        def _():
            inv = (ab[:, CHI:] * (unscale * RIGHT_SCALE)).astype(BF16)
            for t in range(LEVELS):
                put_level(wide, t, dot(inv, q[:, t * CHI : (t + 1) * CHI]))
            for h in range(2):
                out[:, h * 128 : (h + 1) * 128] = wide[h].astype(BF16)

    @pl.when(jnp.logical_not(busy))
    def _():
        @pl.when(is_left)
        def _():
            for x in range(2):
                out[x * HALF : (x + 1) * HALF, :] = owns[x][...]

        @pl.when(jnp.logical_not(is_left))
        def _():
            for h in range(2):
                for u in range(LEVELS // 2):
                    for e in range(2):
                        slab = owns[h][u * CHI : (u + 1) * CHI, e * 128 : (e + 1) * 128].astype(F32)
                        wide[h, pl.ds(2 * u + e, CHI, stride=LEVELS), :] = slab
            for h in range(2):
                out[:, h * 128 : (h + 1) * 128] = wide[h].astype(BF16)


HALF_ARRAY = jax.ShapeDtypeStruct((HALF, CHI), BF16)
WHOLE = pltpu.VMEM((ROWS, CHI), BF16)
TURNED = pltpu.VMEM((CHI, ROWS), BF16)
WIDE = pltpu.VMEM((2, ROWS, 128), F32)
GRAM = pltpu.VMEM((CHI, 2 * CHI), F32)
FACTOR = [WHOLE, TURNED, WIDE, TURNED, GRAM]
HALF_SCRATCH = [pltpu.VMEM((HALF, CHI), BF16), pltpu.VMEM((BONDS, GATE, CHI), BF16)]


def call(kernel, name, out_shape, scratch, limit, *args, aliases={}):
    single = not isinstance(out_shape, tuple)
    return pl.pallas_call(
        kernel,
        out_shape=out_shape,
        in_specs=[VMEM] * len(args),
        out_specs=VMEM if single else tuple(VMEM for _ in out_shape),
        scratch_shapes=scratch,
        input_output_aliases=aliases,
        compiler_params=pltpu.CompilerParams(vmem_limit_bytes=limit << 20),
        name=name,
    )(*args)


def per_device(site_tensors, first_gates, second_gates, first_sketch, second_sketch):
    devices = lax.axis_size("site")
    inside = [(i, i ^ 1) for i in range(devices)]
    across = [(i, (i + 1) % devices if i % 2 else (i - 1) % devices) for i in range(devices)]
    product_scratch = [pltpu.VMEM((2, HALF, CHI), BF16), WIDE]
    whole_matrix = jax.ShapeDtypeStruct((ROWS, ROWS), BF16)
    half_matrix = jax.ShapeDtypeStruct((HALF, ROWS), BF16)
    whole_array = jax.ShapeDtypeStruct((ROWS, CHI), BF16)
    partial = jax.ShapeDtypeStruct((ROWS, CHI), F32)
    gate_shape = jax.ShapeDtypeStruct((4 * GATE, 4 * GATE), BF16)
    gate_rows_shape = jax.ShapeDtypeStruct((GATE, CHI), BF16)
    product_shape = jax.ShapeDtypeStruct((CHI, GATE, CHI), BF16)
    own = site_tensors[0].reshape(ROWS, CHI)
    recv = lax.ppermute(own, "site", inside)
    gate_recv = lax.ppermute(first_gates[0], "site", inside)
    sk1 = second_sketch[0].astype(BF16)
    sk0, recv, gate_recv, sk1 = lax.optimization_barrier((first_sketch[0], recv, gate_recv, sk1))
    sk0_recv = lax.ppermute(sk0, "site", inside)
    y, gate, gate_rows = call(
        early_kernel,
        "early",
        (product_shape, gate_shape, gate_rows_shape),
        product_scratch,
        24,
        own,
        recv,
        first_gates[0],
        gate_recv,
        second_gates[0],
    )
    sk1 = jnp.concatenate([sk1, gate_rows], axis=0)
    sk1_recv = lax.ppermute(sk1, "site", across)
    _, _, m = call(
        late_kernel,
        "late",
        (product_shape, gate_shape, whole_matrix),
        product_scratch,
        24,
        y,
        gate,
        own,
        recv,
        first_gates[0],
        gate_recv,
        aliases={0: 0, 1: 1},
    )
    own_a, own_b = call(first_kernel, "first", (HALF_ARRAY, HALF_ARRAY), [WHOLE, *FACTOR], 24, m, sk0, sk0_recv)
    recv_a = lax.ppermute(own_a, "site", across)
    recv_b = lax.ppermute(own_b, "site", across)
    sk, gate = call(ready_kernel, "ready", (whole_array, gate_shape), [], 8, sk1, sk1_recv)
    acc, s0, m0 = call(
        mid_kernel, "mid", (partial, HALF_ARRAY, half_matrix), HALF_SCRATCH, 24, own_a, own_b, recv_a, sk, gate
    )
    last_scratch = [*HALF_SCRATCH, pltpu.VMEM((HALF, ROWS), BF16), *FACTOR]
    made = call(
        last_kernel, "last", whole_array, last_scratch, 32, own_a, own_b, recv_b, sk, gate, acc, s0, m0
    )
    return made.reshape(1, CHI, LEVELS, CHI)


def solution(mesh):
    in_specs = (
        P("site", None, None, None),
        P("site", None, None),
        P("site", None, None),
        P("site", None, None),
        P("site", None, None),
    )
    out_specs = P("site", None, None, None)
    return jax.shard_map(
        per_device, mesh=mesh, in_specs=in_specs, out_specs=out_specs, check_vma=False
    )
```

```python
import jax
import jax.numpy as jnp
from jax import lax
from jax.experimental import pallas as pl
from jax.experimental.pallas import tpu as pltpu
from jax.sharding import PartitionSpec as P

F32 = jnp.float32
BF16 = jnp.bfloat16
VMEM = pl.BlockSpec(memory_space=pltpu.VMEM)
CHI = 256
LEVELS = 8
ROWS = CHI * LEVELS
GATE = LEVELS * LEVELS
BLOCK = 64


def lanes_of(v, k):
    return jnp.broadcast_to(v[:, k : k + 1], (8, 128))


def row_of(v, r):
    return jnp.broadcast_to(v[r : r + 1, :], (8, 128))


def inverse_factor(diag_block):
    nb = BLOCK
    nv = nb // 8
    rows = lax.broadcasted_iota(jnp.int32, (nb, nb), 0)
    cols = lax.broadcasted_iota(jnp.int32, (nb, nb), 1)
    beside = jnp.concatenate([diag_block, jnp.where(rows == cols, 1.0, 0.0).astype(F32)], axis=1)
    v = [beside[8 * q : 8 * q + 8, :] for q in range(nv)]
    sub = lax.broadcasted_iota(jnp.int32, (8, 128), 0)
    scale = [jnp.ones((8, 128), F32)] * nv
    c = [[lanes_of(v[q], i) for q in range(nv)] for i in range(4)]
    for k in range(0, nb, 4):
        p, r = divmod(k, 8)
        last = k + 4 >= nb
        if not last:
            p2, r2 = divmod(k + 4, 8)
            ahead = [[lanes_of(v[q], k + 4 + i) for q in range(p2, nv)] for i in range(4)]
        row = [row_of(v[p], r + i) for i in range(4)]
        g = [[row_of(c[j][0], r + i) if i >= j else None for j in range(4)] for i in range(4)]
        a, b, d = g[0][0], g[1][0], g[1][1]
        det = a * d - b * b
        idet = 1.0 / det

        def adjugate(x, y):
            return x * d - y * b, y * a - x * b

        n20, n21 = adjugate(g[2][0], g[2][1])
        n30, n31 = adjugate(g[3][0], g[3][1])
        a2 = g[2][2] - (g[2][0] * n20 + g[2][1] * n21) * idet
        b2 = g[3][2] - (g[3][0] * n20 + g[3][1] * n21) * idet
        d2 = g[3][3] - (g[3][0] * n30 + g[3][1] * n31) * idet
        det2 = a2 * d2 - b2 * b2
        idet2 = 1.0 / det2
        m20, m21, m30, m31 = n20 * idet, n21 * idet, n30 * idet, n31 * idet

        def panel_solve(x0, x1, x2, x3):
            u0, u1 = adjugate(x0, x1)
            y2 = x2 - (m20 * x0 + m21 * x1)
            y3 = x3 - (m30 * x0 + m31 * x1)
            return u0 * idet, u1 * idet, (y2 * d2 - y3 * b2) * idet2, (y3 * a2 - y2 * b2) * idet2, y2, y3

        ce = [
            (
                c[0][q - p],
                c[1][q - p],
                c[2][q - p] - (m20 * c[0][q - p] + m21 * c[1][q - p]),
                c[3][q - p] - (m30 * c[0][q - p] + m31 * c[1][q - p]),
            )
            for q in range(p, nv)
        ]
        if not last:
            across = panel_solve(*[c[j][p2 - p] for j in range(4)])[:4]
            c_next = []
            for i in range(4):
                hs = [row_of(x, r2 + i) for x in across]
                c_next.append(
                    [
                        (ahead[i][q - p2] - (ce[q - p][0] * hs[0] + ce[q - p][1] * hs[1]))
                        - (ce[q - p][2] * hs[2] + ce[q - p][3] * hs[3])
                        for q in range(p2, nv)
                    ]
                )
        u0, u1, h2, h3, row2, row3 = panel_solve(*row)
        below = sub > r + 3
        for q in range(p, nv):
            cq = ce[q - p]
            if q == p:
                cq = [jnp.where(below, x, 0.0) for x in cq]
            v[q] = (v[q] - (cq[0] * u0 + cq[1] * u1)) - (cq[2] * h2 + cq[3] * h3)
        ia = 1.0 / a
        ia2 = 1.0 / a2
        row1 = row[1] - (b * ia) * row[0]
        row3 = row3 - (b2 * ia2) * row2
        v[p] = jnp.where(
            sub == r + 1, row1, jnp.where(sub == r + 2, row2, jnp.where(sub == r + 3, row3, v[p]))
        )
        scale[p] = jnp.where(
            sub == r,
            lax.rsqrt(a),
            jnp.where(
                sub == r + 1,
                lax.rsqrt(det * ia),
                jnp.where(sub == r + 2, lax.rsqrt(a2), jnp.where(sub == r + 3, lax.rsqrt(det2 * ia2), scale[p])),
            ),
        )
        if not last:
            c = c_next
    return jnp.concatenate([v[q] * scale[q] for q in range(nv)], axis=0)


def dot(x, y, dims=((1,), (0,))):
    return lax.dot_general(x, y, (dims, ((), ())), preferred_element_type=F32)


def dot_split(x, y, dims=((1,), (0,))):
    xh = x.astype(BF16)
    xl = (x - xh.astype(F32)).astype(BF16)
    yh = y.astype(BF16)
    yl = (y - yh.astype(F32)).astype(BF16)
    return dot(xh, yh, dims) + (dot(xh, yl, dims) + dot(xl, yh, dims))


def gate_matrix(packed):
    i = lax.broadcasted_iota(jnp.int32, (GATE, GATE), 0)
    j = lax.broadcasted_iota(jnp.int32, (GATE, GATE), 1)
    swap = jnp.where(j == (i & 7) * 8 + (i >> 3), 1.0, 0.0).astype(BF16)
    g = dot(dot(swap, packed[:, :GATE]).astype(BF16), swap, ((1,), (1,))).astype(BF16)
    wide = jnp.concatenate([jnp.concatenate([g] * 4, axis=1)] * 4, axis=0)
    big_i = lax.broadcasted_iota(jnp.int32, (4 * GATE, 4 * GATE), 0)
    big_j = lax.broadcasted_iota(jnp.int32, (4 * GATE, 4 * GATE), 1)
    return jnp.where((big_i >> 6) == (big_j >> 6), wide, jnp.zeros_like(wide))


HALF = ROWS // 2
ROW_SITES = 32
BONDS = CHI // 2
STEP = 512


def put_level(wide, t, value):
    for h in range(2):
        wide[h, pl.ds(t, CHI, stride=LEVELS), :] = value[:, h * 128 : (h + 1) * 128]


def take_slabs(wide, put):
    for h in range(2):
        for u in range(LEVELS // 2):
            pair = [wide[h, pl.ds(2 * u + e, CHI, stride=LEVELS), :] for e in range(2)]
            put(h, u, jnp.concatenate(pair, axis=1).astype(BF16))


def identity(dtype):
    i = lax.broadcasted_iota(jnp.int32, (CHI, CHI), 0)
    j = lax.broadcasted_iota(jnp.int32, (CHI, CHI), 1)
    return jnp.where(i == j, 1.0, 0.0).astype(dtype)


def two_site(lhs_of, weights_of, y, a0):
    for p in range(2):
        block, weights = lhs_of(p), weights_of(p)
        for u in range(LEVELS // 2):
            made = dot(block, weights[u * CHI : (u + 1) * CHI, :]).reshape(BONDS, LEVELS, CHI)
            both = jnp.concatenate([made[:, :, :128], made[:, :, 128:]], axis=1).astype(BF16)
            y[pl.ds(a0, BONDS), 16 * u : 16 * u + 16, p * 128 : (p + 1) * 128] = both


def gated(y, gate, m, rows):
    bonds = STEP // LEVELS

    def some(i, _):
        r0 = pl.multiple_of(i * STEP, STEP)
        a0 = pl.multiple_of(i * bonds, bonds)
        for j in range(bonds // 4):
            four = y[pl.ds(a0 + 4 * j, 4)].reshape(4 * GATE, CHI)
            o = dot(gate[...], four).reshape(4, LEVELS, LEVELS, CHI)
            for h in range(2):
                at = pl.multiple_of(r0 + j * 32 + h * 16, 16)
                for t in range(LEVELS):
                    m[pl.ds(at, 16), t * CHI : (t + 1) * CHI] = jnp.concatenate(
                        [o[2 * h, t], o[2 * h + 1, t]], axis=0
                    ).astype(BF16)
        return 0

    lax.fori_loop(0, rows // STEP, some, 0)


def factor(ab, alongside):
    unit = identity(F32)
    gram = ab[:, :CHI]
    largest = jnp.max(gram * unit, keepdims=True)
    ab[:, :CHI] = gram * (1.0 / largest)
    ab[:, CHI:] = unit
    lane = lax.broadcasted_iota(jnp.int32, (BLOCK, 128), 1)
    none = jnp.zeros((BLOCK, 2 * CHI), F32)
    block = ab[:BLOCK, :BLOCK]
    for o in range(0, CHI, BLOCK):
        e = o + BLOCK
        uw = inverse_factor(block)
        alongside(o // BLOCK)
        panel = dot_split(uw, jnp.concatenate([none, ab[o:e, :]], axis=0))
        ab[o:e, CHI:] = panel[:, CHI:]
        if e < CHI:
            tile = o // 128 * 128
            if o == tile:
                w = jnp.concatenate([uw[:, BLOCK:], jnp.zeros((BLOCK, BLOCK), F32)], axis=1)
            else:
                w = jnp.where(lane >= BLOCK, uw, 0.0)
            turned = dot_split(ab[e:, tile : tile + 128], w, ((1,), (1,)))
            top = ab[e : e + BLOCK, :] - dot_split(turned[:BLOCK], panel)
            block = top[:, e : e + BLOCK]
            ab[e : e + BLOCK, :] = top
            if e + BLOCK < CHI:
                ab[e + BLOCK :, :] = ab[e + BLOCK :, :] - dot_split(turned[BLOCK:], panel)
    return lax.rsqrt(largest)


LEFT_SCALE = LEVELS**0.5 * CHI**0.25
RIGHT_SCALE = LEFT_SCALE * ROWS**-0.5


def waits_long():
    return lax.rem(lax.axis_index("site"), ROW_SITES) == 0


def product(left, right, y, wts, wide):
    for h in range(2):
        wide[h] = right[:, h * 128 : (h + 1) * 128].astype(F32)

    def put(h, u, value):
        wts[h, u * CHI : (u + 1) * CHI, :] = value

    take_slabs(wide, put)

    def some(x, _):
        block = left[pl.ds(pl.multiple_of(x * HALF, HALF), HALF), :]
        two_site(lambda p: block, lambda p: wts.at[p], y, pl.multiple_of(x * BONDS, BONDS))
        return 0

    lax.fori_loop(0, 2, some, 0)


def early_kernel(own, recv, gate_recv, gate_next, y, gate_rows, wts, wide):
    gate_rows[...] = jnp.concatenate([gate_next[...]] * 4, axis=1)

    @pl.when(waits_long())
    def _():
        product(own, recv, y, wts, wide)


def late_kernel(y_in, own, recv, gate_own, gate_recv, y, m, gate, wts, wide):
    is_left = lax.rem(lax.axis_index("site"), 2) == 0

    @pl.when(jnp.logical_not(waits_long()))
    def _():
        @pl.when(is_left)
        def _():
            gate[...] = gate_matrix(gate_own[...])
            product(own, recv, y, wts, wide)

        @pl.when(jnp.logical_not(is_left))
        def _():
            gate[...] = gate_matrix(gate_recv[...])
            product(recv, own, y, wts, wide)

    @pl.when(waits_long())
    def _():
        gate[...] = gate_matrix(gate_own[...])

    gated(y, gate, m, ROWS)


def first_kernel(m, sk_own, sk_recv, out_a, out_b, s, st, wide, q, ab):
    is_left = lax.rem(lax.axis_index("site"), 2) == 0
    outs = (out_a, out_b)

    def sample(sketch):
        def some(i, _):
            rows = pl.ds(pl.multiple_of(i * HALF, HALF), HALF)
            s[rows, :] = dot(m[rows, :], sketch[:ROWS, :]).astype(BF16)
            return 0

        lax.fori_loop(0, 2, some, 0)

    @pl.when(is_left)
    def _():
        sample(sk_own)

    @pl.when(jnp.logical_not(is_left))
    def _():
        sample(sk_recv)

    st[...] = dot(identity(BF16), s[...], ((1,), (1,))).astype(BF16)
    ab[:, :CHI] = dot(st[...], s[...])

    def alongside(j):
        for t in (2 * j, 2 * j + 1):
            q[:, t * CHI : (t + 1) * CHI] = dot(st[...], m[:, t * CHI : (t + 1) * CHI]).astype(BF16)

    unscale = factor(ab, alongside)

    @pl.when(is_left)
    def _():
        made = dot(s[...], (ab[:, CHI:] * (unscale * LEFT_SCALE)).astype(BF16), ((1,), (1,)))
        for h in range(2):
            wide[h] = made[:, h * 128 : (h + 1) * 128]

        def put_out(h, u, value):
            outs[h][u * CHI : (u + 1) * CHI, :] = value

        take_slabs(wide, put_out)

    @pl.when(jnp.logical_not(is_left))
    def _():
        inv = (ab[:, CHI:] * (unscale * RIGHT_SCALE)).astype(BF16)
        for t in range(LEVELS):
            put_level(wide, t, dot(inv, q[:, t * CHI : (t + 1) * CHI]))
        for x in range(2):
            for h in range(2):
                outs[x][:, h * 128 : (h + 1) * 128] = wide[h, x * HALF : (x + 1) * HALF, :].astype(BF16)


def ready_kernel(sk_own, sk_recv, sk, gate):
    is_left, _ = role()

    def take(packed):
        sk[...] = packed[:ROWS, :]
        gate[...] = gate_matrix(packed[ROWS:, :])

    @pl.when(is_left)
    def _():
        take(sk_own)

    @pl.when(jnp.logical_not(is_left))
    def _():
        take(sk_recv)


def half_pair(own_a, own_b, recv, gate, y, m, is_left):
    owns = (own_a, own_b)

    @pl.when(is_left)
    def _():
        two_site(lambda p: owns[p][...], lambda p: recv, y, 0)

    @pl.when(jnp.logical_not(is_left))
    def _():
        block = recv[...]
        two_site(lambda p: block, lambda p: owns[p], y, 0)

    gated(y, gate, m, HALF)


def column_half(sk, sh, h):
    for t in range(LEVELS):
        at = t * CHI + h * 128
        sh[t * 128 : (t + 1) * 128, :] = sk[at : at + 128, :]


def sampled_rows(m, sh, g):
    lanes = [m[:, t * CHI + g * 128 : t * CHI + (g + 1) * 128] for t in range(LEVELS)]
    return dot(jnp.concatenate(lanes, axis=1), sh[...])


def role():
    me = lax.axis_index("site")
    return lax.rem(me, 2) == 1, (me > 0) & (me < lax.axis_size("site") - 1)


def mid_kernel(own_a, own_b, recv, sk, gate, acc, s0, m, sh, y):
    is_left, busy = role()

    @pl.when(busy)
    def _():
        half_pair(own_a, own_b, recv, gate, y, m, is_left)

        @pl.when(is_left)
        def _():
            column_half(sk, sh, 0)
            for g in range(2):
                acc[g * HALF : (g + 1) * HALF, :] = sampled_rows(m, sh, g)
            s0[...] = jnp.zeros_like(s0)

        @pl.when(jnp.logical_not(is_left))
        def _():
            s0[...] = dot(m[...], sk[...]).astype(BF16)


def last_kernel(
    own_a, own_b, recv, sk, gate, acc, s0, m0, out, sh, y, m, s, st, wide, q, ab
):
    is_left, busy = role()
    owns = (own_a, own_b)

    @pl.when(busy)
    def _():
        half_pair(own_a, own_b, recv, gate, y, m, is_left)

        @pl.when(is_left)
        def _():
            column_half(sk, sh, 1)
            for g in range(2):
                rows = slice(g * HALF, (g + 1) * HALF)
                s[rows, :] = (acc[rows, :] + sampled_rows(m, sh, g)).astype(BF16)

        @pl.when(jnp.logical_not(is_left))
        def _():
            s[:HALF, :] = s0[...]
            s[HALF:, :] = dot(m[...], sk[...]).astype(BF16)

        st[...] = dot(identity(BF16), s[...], ((1,), (1,))).astype(BF16)
        ab[:, :CHI] = dot(st[...], s[...])

        def alongside(j):
            for t in (2 * j, 2 * j + 1):
                columns = slice(t * CHI, (t + 1) * CHI)
                made = dot(st[:, :HALF], m0[:, columns]) + dot(st[:, HALF:], m[:, columns])
                q[:, columns] = made.astype(BF16)

        unscale = factor(ab, alongside)

        @pl.when(is_left)
        def _():
            out[...] = dot(s[...], (ab[:, CHI:] * (unscale * LEFT_SCALE)).astype(BF16), ((1,), (1,))).astype(BF16)

        @pl.when(jnp.logical_not(is_left))
        def _():
            inv = (ab[:, CHI:] * (unscale * RIGHT_SCALE)).astype(BF16)
            for t in range(LEVELS):
                put_level(wide, t, dot(inv, q[:, t * CHI : (t + 1) * CHI]))
            for h in range(2):
                out[:, h * 128 : (h + 1) * 128] = wide[h].astype(BF16)

    @pl.when(jnp.logical_not(busy))
    def _():
        @pl.when(is_left)
        def _():
            for x in range(2):
                out[x * HALF : (x + 1) * HALF, :] = owns[x][...]

        @pl.when(jnp.logical_not(is_left))
        def _():
            for h in range(2):
                for u in range(LEVELS // 2):
                    for e in range(2):
                        slab = owns[h][u * CHI : (u + 1) * CHI, e * 128 : (e + 1) * 128].astype(F32)
                        wide[h, pl.ds(2 * u + e, CHI, stride=LEVELS), :] = slab
            for h in range(2):
                out[:, h * 128 : (h + 1) * 128] = wide[h].astype(BF16)


HALF_ARRAY = jax.ShapeDtypeStruct((HALF, CHI), BF16)
WHOLE = pltpu.VMEM((ROWS, CHI), BF16)
TURNED = pltpu.VMEM((CHI, ROWS), BF16)
WIDE = pltpu.VMEM((2, ROWS, 128), F32)
GRAM = pltpu.VMEM((CHI, 2 * CHI), F32)
FACTOR = [WHOLE, TURNED, WIDE, TURNED, GRAM]
HALF_SCRATCH = [pltpu.VMEM((HALF, CHI), BF16), pltpu.VMEM((BONDS, GATE, CHI), BF16)]


def call(kernel, name, out_shape, scratch, limit, *args, aliases={}):
    single = not isinstance(out_shape, tuple)
    return pl.pallas_call(
        kernel,
        out_shape=out_shape,
        in_specs=[VMEM] * len(args),
        out_specs=VMEM if single else tuple(VMEM for _ in out_shape),
        scratch_shapes=scratch,
        input_output_aliases=aliases,
        compiler_params=pltpu.CompilerParams(vmem_limit_bytes=limit << 20),
        name=name,
    )(*args)


def per_device(site_tensors, first_gates, second_gates, first_sketch, second_sketch):
    devices = lax.axis_size("site")
    inside = [(i, i ^ 1) for i in range(devices)]
    across = [(i, (i + 1) % devices if i % 2 else (i - 1) % devices) for i in range(devices)]
    product_scratch = [pltpu.VMEM((2, HALF, CHI), BF16), WIDE]
    whole_matrix = jax.ShapeDtypeStruct((ROWS, ROWS), BF16)
    half_matrix = jax.ShapeDtypeStruct((HALF, ROWS), BF16)
    whole_array = jax.ShapeDtypeStruct((ROWS, CHI), BF16)
    partial = jax.ShapeDtypeStruct((ROWS, CHI), F32)
    gate_shape = jax.ShapeDtypeStruct((4 * GATE, 4 * GATE), BF16)
    gate_rows_shape = jax.ShapeDtypeStruct((GATE, CHI), BF16)
    product_shape = jax.ShapeDtypeStruct((CHI, GATE, CHI), BF16)
    own = site_tensors[0].reshape(ROWS, CHI)
    recv = lax.ppermute(own, "site", inside)
    gate_recv = lax.ppermute(first_gates[0], "site", inside)
    sk0 = first_sketch[0].astype(BF16)
    sk0_recv = lax.ppermute(sk0, "site", inside)
    y, gate_rows = call(
        early_kernel,
        "early",
        (product_shape, gate_rows_shape),
        product_scratch,
        24,
        own,
        recv,
        gate_recv,
        second_gates[0],
    )
    sk1 = jnp.concatenate([second_sketch[0].astype(BF16), gate_rows], axis=0)
    sk1_recv = lax.ppermute(sk1, "site", across)
    _, m = call(
        late_kernel,
        "late",
        (product_shape, whole_matrix),
        [pltpu.VMEM((4 * GATE, 4 * GATE), BF16), *product_scratch],
        24,
        y,
        own,
        recv,
        first_gates[0],
        gate_recv,
        aliases={0: 0},
    )
    own_a, own_b = call(first_kernel, "first", (HALF_ARRAY, HALF_ARRAY), FACTOR, 24, m, sk0, sk0_recv)
    recv_a = lax.ppermute(own_a, "site", across)
    recv_b = lax.ppermute(own_b, "site", across)
    sk, gate = call(ready_kernel, "ready", (whole_array, gate_shape), [], 8, sk1, sk1_recv)
    acc, s0, m0 = call(
        mid_kernel, "mid", (partial, HALF_ARRAY, half_matrix), HALF_SCRATCH, 24, own_a, own_b, recv_a, sk, gate
    )
    last_scratch = [*HALF_SCRATCH, pltpu.VMEM((HALF, ROWS), BF16), *FACTOR]
    made = call(
        last_kernel, "last", whole_array, last_scratch, 32, own_a, own_b, recv_b, sk, gate, acc, s0, m0
    )
    return made.reshape(1, CHI, LEVELS, CHI)


def solution(mesh):
    in_specs = (
        P("site", None, None, None),
        P("site", None, None),
        P("site", None, None),
        P("site", None, None),
        P("site", None, None),
    )
    out_specs = P("site", None, None, None)
    return jax.shard_map(
        per_device, mesh=mesh, in_specs=in_specs, out_specs=out_specs, check_vma=False
    )
```
